512 devices in a mesh: dp: 32 (over y, z_lo), seq: 16 (over z_hi, x, core).
Axes of the slice: x: 4, y: 4, z: 16 (z_hi: 2, z_lo: 8; z = z_hi * 8 + z_lo), core: 2. Of those that a mesh axis runs over, the one named last changes fastest.
Arguments:
- signal: bfloat16 [32, 2048, 768], P('dp', 'seq'), may hold values from -6 to 6
- norm_gain: float32 [768], replicated, may hold values from 0.1 to 1.9
- conv_taps: float32 [5, 768], replicated, may hold values from -3 to 3
- w_query: bfloat16 [768, 768], replicated, may hold values from -1 to 1
- w_key: bfloat16 [768, 768], replicated, may hold values from -8 to 8
- w_value: bfloat16 [768, 768], replicated, may hold values from -0.21875 to 0.21875
- cotangent: bfloat16 [32, 2048, 768], P('dp', 'seq'), may hold values from -6 to 6
Outputs:
- grad_signal: bfloat16 [32, 2048, 768], P('dp', 'seq')
- grad_taps: float32 [5, 768], replicated
- grad_gain: float32 [768], replicated
The draws below stay inside these ranges and needn't reach their ends.
All inputs are finite; a program needn't handle non-finite values.
Results may differ from the reference program's by a relative error of at most 0.035.
Values may be sent and summed in bfloat16 or wider, within the bound.
No kernel may reach another device: no remote copies, remote signals or barrier semaphores. Data moves between devices by JAX's collectives and lax.ppermute only.
A program may use at most 128 MiB of HBM per device.

```python
import math
import jax
import jax.numpy as jnp
from jax import lax

C = 768
HEADS = 6
HEAD_DIM = 128
ATT = 768
WIN = 5
BIN_DEV = 128
BINS = 2048
SEQS = 32


def paired_weights(key):
    base_key = jax.random.fold_in(key, 11)
    other_key = jax.random.fold_in(key, 12)
    clip_at = 6.0
    first = jnp.clip(jax.random.normal(base_key, (C, ATT), jnp.float32), -clip_at, clip_at) / math.sqrt(C)
    second = jnp.clip(jax.random.normal(other_key, (C, ATT), jnp.float32), -clip_at, clip_at) / math.sqrt(C)
    return (first, jnp.clip(second, -8.0, 8.0))


def draw_w_query(key, part):
    return paired_weights(key)[0].astype(jnp.bfloat16)


def draw_w_key(key, part):
    return paired_weights(key)[1].astype(jnp.bfloat16)


def steps_of(own_key, shape, shards, least, largest):
    gain, own = 1.0, jax.random.fold_in(own_key, 6)
    for dim, shards_of in shards:
        steps = jnp.exp(jax.random.uniform(jax.random.fold_in(own, dim), (shards_of,), jnp.float32, least / len(shards), largest / len(shards)))
        gain = gain * jnp.repeat(steps, shape[dim] // shards_of).reshape([-1 if axis == dim else 1 for axis in range(len(shape))])
    return gain


def bell_draw(rng, extent, width, reach, split=(), kind=jnp.bfloat16):
    factor_of = steps_of(rng, extent, split, -0.22, 0.18) if split else 1.0
    values = jax.random.normal(rng, extent, jnp.float32) * width * factor_of
    return jnp.minimum(jnp.maximum(values, -reach), reach).astype(kind)


def setup_inputs(seed: int = 0) -> dict:
    arg_keys = jax.random.split(jax.random.key(seed), 8)
    signal = bell_draw(arg_keys[0], (SEQS, BINS, C), 1.0, 6.0, ((0, 32), (1, 16)))
    norm_gain = jnp.clip(1.0 + 0.18 * jax.random.normal(arg_keys[1], (C,), jnp.float32), 0.1, 1.9)
    conv_taps = bell_draw(arg_keys[2], (WIN, C), 0.5, 3.0, (), jnp.float32)
    w_query = draw_w_query(jax.random.fold_in(arg_keys[7], 71), 0)
    w_key = draw_w_key(jax.random.fold_in(arg_keys[7], 71), 0)
    w_value = bell_draw(arg_keys[5], (C, ATT), C ** -0.5, 0.21875)
    cotangent = bell_draw(arg_keys[6], (SEQS, BINS, ATT), 1.0, 6.0, ((0, 32), (1, 16)))
    return dict(signal=signal, norm_gain=norm_gain, conv_taps=conv_taps, w_query=w_query, w_key=w_key, w_value=w_value, cotangent=cotangent)


EPSILON = 1e-06
GELU_ROOT = math.sqrt(2.0 / math.pi)

def gelu_pair(inputs):
    inner = GELU_ROOT * (inputs + 0.044715 * inputs * inputs * inputs)
    tangent = jnp.tanh(inner)
    output = 0.5 * inputs * (1.0 + tangent)
    derivative = 0.5 * (1.0 + tangent) + 0.5 * inputs * (1.0 - tangent * tangent) * GELU_ROOT * (1.0 + 3.0 * 0.044715 * inputs * inputs)
    return (output, derivative)

def reference(signal, norm_gain, conv_taps, w_query, w_key, w_value, cotangent):
    score_scale = 1.0 / math.sqrt(HEAD_DIM)
    margin = WIN // 2
    wide_in = signal.astype(jnp.float32)
    inv_rms = lax.rsqrt(lax.optimization_barrier(jnp.mean(wide_in * wide_in, axis=-1, keepdims=True)) + EPSILON)
    normed = wide_in * inv_rms * norm_gain
    padded = jnp.pad(normed, ((0, 0), (margin, margin), (0, 0)))
    conv_out = jnp.zeros_like(normed)
    for offset in range(WIN):
        conv_out = conv_out + conv_taps[offset] * padded[:, offset:offset + BINS]
    active, gelu_slope = gelu_pair(conv_out)
    hidden = (wide_in + active).astype(jnp.bfloat16)
    flat_hidden = hidden.reshape(SEQS * BINS, C)

    def project(weight):
        result = jnp.dot(flat_hidden, weight, preferred_element_type=jnp.float32).astype(jnp.bfloat16)
        return result.reshape(SEQS, BINS, HEADS, HEAD_DIM)
    queries = project(w_query)
    keys_all = project(w_key)
    values_all = project(w_value)
    grads_out = cotangent.reshape(SEQS, BINS, HEADS, HEAD_DIM)
    block_count = BINS // BIN_DEV

    def one_sequence(operands):
        query_seq, key_seq, value_seq, grad_seq = operands
        key_wide = key_seq.astype(jnp.float32)
        value_wide = value_seq.astype(jnp.float32)

        def block_scores(query_block):
            return jnp.einsum('qhd,khd->hqk', query_block.astype(jnp.float32), key_wide) * score_scale

        def forward_block(query_block):
            scores = block_scores(query_block)
            row_max = lax.optimization_barrier(jnp.max(scores, axis=-1, keepdims=True))
            exp_scores = jnp.exp(scores - row_max)
            row_total = lax.optimization_barrier(jnp.sum(exp_scores, axis=-1, keepdims=True))
            weights = (exp_scores / row_total).astype(jnp.bfloat16)
            attended = jnp.einsum('hqk,khd->qhd', weights.astype(jnp.float32), value_wide).astype(jnp.bfloat16)
            return (attended, (row_max + jnp.log(row_total))[..., 0])
        query_blocks = query_seq.reshape(block_count, BIN_DEV, HEADS, HEAD_DIM)
        grad_blocks = grad_seq.reshape(block_count, BIN_DEV, HEADS, HEAD_DIM)
        attended_blocks, log_totals = lax.map(forward_block, query_blocks)

        def backward_block(running, operands_block):
            query_block, grad_block, attended_block, log_total = operands_block
            scores = block_scores(query_block)
            probs = jnp.exp(scores - log_total[..., None])
            row_delta = lax.optimization_barrier(jnp.sum(grad_block.astype(jnp.float32) * attended_block.astype(jnp.float32), axis=-1))
            dprob = jnp.einsum('qhd,khd->hqk', grad_block.astype(jnp.float32), value_wide)
            dscore = (probs * (dprob - row_delta.T[:, :, None])).astype(jnp.bfloat16)
            grad_query = (jnp.einsum('hqk,khd->qhd', dscore.astype(jnp.float32), key_wide) * score_scale).astype(jnp.bfloat16)
            key_part = (jnp.einsum('hqk,qhd->khd', dscore.astype(jnp.float32), query_block.astype(jnp.float32)) * score_scale).astype(jnp.bfloat16)
            value_part = jnp.einsum('hqk,qhd->khd', probs.astype(jnp.bfloat16).astype(jnp.float32), grad_block.astype(jnp.float32)).astype(jnp.bfloat16)
            return ((running[0] + key_part.astype(jnp.float32), running[1] + value_part.astype(jnp.float32)), grad_query)
        zeros_init = jnp.zeros((BINS, HEADS, HEAD_DIM), jnp.float32)
        sums, grad_query = lax.scan(backward_block, (zeros_init, zeros_init), (query_blocks, grad_blocks, attended_blocks, log_totals))
        return (grad_query.reshape(BINS, ATT), sums[0].astype(jnp.bfloat16).reshape(BINS, ATT), sums[1].astype(jnp.bfloat16).reshape(BINS, ATT))
    grad_query, grad_key, grad_value = lax.map(one_sequence, (queries, keys_all, values_all, grads_out))
    grad_hidden = jnp.dot(grad_query.reshape(-1, ATT), w_query.T, preferred_element_type=jnp.float32)
    grad_hidden = grad_hidden + jnp.dot(grad_key.reshape(-1, ATT), w_key.T, preferred_element_type=jnp.float32)
    grad_hidden = grad_hidden + jnp.dot(grad_value.reshape(-1, ATT), w_value.T, preferred_element_type=jnp.float32)
    grad_hidden = grad_hidden.reshape(SEQS, BINS, C)
    grad_conv = grad_hidden * gelu_slope
    grad_padded = jnp.pad(grad_conv, ((0, 0), (margin, margin), (0, 0)))
    tap_rows = []
    grad_normed = jnp.zeros_like(grad_conv)
    for offset in range(WIN):
        tap_rows.append(lax.optimization_barrier(jnp.sum(grad_conv * padded[:, offset:offset + BINS], axis=(0, 1))))
        start_at = 2 * margin - offset
        grad_normed = grad_normed + conv_taps[offset] * grad_padded[:, start_at:start_at + BINS]
    grad_taps = jnp.stack(tap_rows)
    grad_gain = lax.optimization_barrier(jnp.sum(grad_normed * wide_in * inv_rms, axis=(0, 1)))
    scaled = grad_normed * norm_gain
    grad_signal = grad_hidden + inv_rms * scaled - wide_in * inv_rms * inv_rms * inv_rms * lax.optimization_barrier(jnp.mean(scaled * wide_in, axis=-1, keepdims=True))
    return (grad_signal.astype(jnp.bfloat16), grad_taps, grad_gain)
```

```python
import math

import jax
import jax.numpy as jnp
from jax import lax
from jax.experimental import pallas as pl
from jax.experimental.pallas import tpu as pltpu
from jax.sharding import Mesh
from jax.sharding import PartitionSpec as P

HEADS = 6
HEAD_DIM = 128
OWN_HEADS = 3
HALF = OWN_HEADS * HEAD_DIM
EPSILON = 1e-06
GELU_ROOT = math.sqrt(2.0 / math.pi)
SCALE = 1.0 / math.sqrt(HEAD_DIM)
BLOCK = 128
CHUNK = 256
CHUNKS = 8
BINS = 2048
C = 768
INTERPRET = False
F32 = jnp.float32
BF16 = jnp.bfloat16
VM = pltpu.VMEM


def vspec():
    return pl.BlockSpec(memory_space=pltpu.VMEM)


def sspec():
    return pl.BlockSpec(memory_space=pltpu.SMEM)


def call(body, out_shape, args, scratch=(), limit=40):
    specs = [sspec() if a.dtype == jnp.int32 else vspec() for a in args]
    outs = jax.tree.map(lambda _: vspec(), out_shape)
    return pl.pallas_call(
        body,
        out_shape=out_shape,
        in_specs=specs,
        out_specs=outs,
        scratch_shapes=list(scratch),
        compiler_params=pltpu.CompilerParams(vmem_limit_bytes=limit << 20),
        interpret=INTERPRET,
    )(*args)


def nt(a, b):
    return lax.dot_general(a, b, (((1,), (1,)), ((), ())), preferred_element_type=F32)


def nn(a, b):
    return lax.dot_general(a, b, (((1,), (0,)), ((), ())), preferred_element_type=F32)


def neighbours(pos, dz, dx):
    zh = pos[0]
    xa = lax.rem(pos[1] + dx, 4)
    za = lax.rem(zh + dz, 2)
    wrap_lo = (xa == 0).astype(jnp.int32)
    wrap_hi = (xa == 3).astype(jnp.int32)
    prev = lax.rem(dz + wrap_lo, 2) * 4 + lax.rem(dx + 3, 4)
    nxt = lax.rem(dz + wrap_hi, 2) * 4 + lax.rem(dx + 1, 4)
    prev_ok = 1 - wrap_lo * (1 - za)
    nxt_ok = 1 - wrap_hi * za
    return prev, nxt, prev_ok.astype(F32), nxt_ok.astype(F32)


def normalize(rows):
    return rows * lax.rsqrt(jnp.mean(rows * rows, axis=-1, keepdims=True) + EPSILON)


def hidden_body(
    pos, s0, s1, s2, s3, s4, s5, s6, s7, e0, e1, w, gain, taps, q, k, v, ext, xs, ns, hs
):
    core = pos[2]
    here = pl.multiple_of(core * BLOCK, BLOCK)
    there = pl.multiple_of((1 - core) * BLOCK, BLOCK)
    for c, s in enumerate((s0, s1, s2, s3, s4, s5, s6, s7)):
        other = e0 if c < 4 else e1
        xs[c, pl.ds(here, BLOCK), :] = s[0:BLOCK, :]
        xs[c, pl.ds(there, BLOCK), :] = other[(c % 4) * BLOCK : (c % 4 + 1) * BLOCK, :]
    prev, nxt, prev_ok, nxt_ok = neighbours(pos, jnp.int32(0), jnp.int32(0))
    first = core == 0
    ext[16:144, :] = s0[0:BLOCK, :]

    @pl.when(first)
    def _():
        ext[0:16, :] = (xs[prev, 240:256, :].astype(F32) * prev_ok).astype(BF16)
        ext[144:160, :] = xs[0, 128:144, :]

    @pl.when(jnp.logical_not(first))
    def _():
        ext[0:16, :] = xs[0, 112:128, :]
        ext[144:160, :] = (xs[nxt, 0:16, :].astype(F32) * nxt_ok).astype(BF16)

    def chunk(c, _):
        dz = lax.div(c, 4)
        dx = lax.rem(c, 4)
        prev, nxt, prev_ok, nxt_ok = neighbours(pos, dz, dx)
        g = gain[0:1, :]
        ns[0:16, :] = normalize(xs[prev, 240:256, :].astype(F32)) * g * prev_ok
        ns[272:288, :] = normalize(xs[nxt, 0:16, :].astype(F32)) * g * nxt_ok
        for r in range(0, CHUNK, 16):
            ns[16 + r : 32 + r, :] = normalize(xs[c, r : r + 16, :].astype(F32)) * g
        for j in range(0, C, 128):
            tap = [taps[t : t + 1, j : j + 128] for t in range(5)]
            for r in range(0, CHUNK, 64):
                u = tap[0] * ns[14 + r : 78 + r, j : j + 128]
                for t in range(1, 5):
                    u = u + tap[t] * ns[14 + r + t : 78 + r + t, j : j + 128]
                inner = GELU_ROOT * (u + 0.044715 * u * u * u)
                act = 0.5 * u * (1.0 + jnp.tanh(inner))
                x = xs[c, r : r + 64, j : j + 128].astype(F32)
                hs[r : r + 64, j : j + 128] = (x + act).astype(BF16)
        y = nn(hs[...], w[...]).astype(BF16)
        at = pl.multiple_of(c * CHUNK, CHUNK)
        for h in range(OWN_HEADS):
            q[h, pl.ds(at, CHUNK), :] = y[:, h * 128 : (h + 1) * 128]
            k[h, pl.ds(at, CHUNK), :] = y[:, HALF + h * 128 : HALF + (h + 1) * 128]
            v[h, pl.ds(at, CHUNK), :] = y[:, 2 * HALF + h * 128 : 2 * HALF + (h + 1) * 128]
        return 0

    lax.fori_loop(0, CHUNKS, chunk, 0)


KB = 512


def forward_body(q, k, v, d0, d4, dq, stats, ds, ss, sm):
    for g, d in enumerate((d0, d4)):
        for h in range(OWN_HEADS):
            ds[h, g * CHUNK : g * CHUNK + BLOCK, :] = d[0:BLOCK, h * 128 : (h + 1) * 128]
            ds[h, g * CHUNK + BLOCK : (g + 1) * CHUNK, :] = d[
                0:BLOCK, HALF + h * 128 : HALF + (h + 1) * 128
            ]
    sm[...] = jnp.zeros_like(sm)
    lane = lax.broadcasted_iota(jnp.int32, (CHUNK, 128), 1)

    def head(h, _):
        for g in range(2):
            qh = q[h, g * 1024 : g * 1024 + CHUNK, :]
            top = None
            for b in range(0, BINS, KB):
                s = nt(qh, k[h, b : b + KB, :])
                ss[:, b : b + KB] = s
                m = jnp.max(s, axis=1, keepdims=True)
                top = m if top is None else jnp.maximum(top, m)
            total = jnp.zeros((CHUNK, 1), F32)
            out = jnp.zeros((CHUNK, HEAD_DIM), F32)
            for b in range(0, BINS, KB):
                p = jnp.exp((ss[:, b : b + KB] - top) * SCALE)
                total = total + jnp.sum(p, axis=1, keepdims=True)
                out = out + nn(p.astype(BF16), v[h, b : b + KB, :])
                if g == 0:
                    ss[:, b : b + KB] = p
            inverse = 1.0 / total
            attended = (out * inverse).astype(BF16).astype(F32)
            do = ds[h, g * CHUNK : (g + 1) * CHUNK, :]
            delta = jnp.sum(do.astype(F32) * attended, axis=1, keepdims=True)
            log_total = top * SCALE + jnp.log(total)
            sl = slice(g * CHUNK, (g + 1) * CHUNK)
            sm[sl, :] = jnp.where(
                lane == h, log_total, jnp.where(lane == h + OWN_HEADS, delta, sm[sl, :])
            )
            if g == 0:
                acc = jnp.zeros((CHUNK, HEAD_DIM), F32)
                for b in range(0, BINS, KB):
                    dp = nt(do, v[h, b : b + KB, :])
                    dsc = (ss[:, b : b + KB] * inverse * (dp - delta)).astype(BF16)
                    acc = acc + nn(dsc, k[h, b : b + KB, :])
                dq[h, :, :] = (acc * SCALE).astype(BF16)
        return 0

    lax.fori_loop(0, OWN_HEADS, head, 0)
    stats[...] = jnp.transpose(sm[...])[0:8, :]


def backward_body(pos, q, k, v, d0, d1, d2, d3, d4, d5, d6, d7, stats, dk, dv, ds):
    for c, d in enumerate((d0, d1, d2, d3, d4, d5, d6, d7)):
        low = BLOCK if c in (1, 2, 3) else 0
        for h in range(OWN_HEADS):
            ds[h, c * CHUNK : c * CHUNK + BLOCK, :] = d[
                low : low + BLOCK, h * 128 : (h + 1) * 128
            ]
            ds[h, c * CHUNK + BLOCK : (c + 1) * CHUNK, :] = d[
                low : low + BLOCK, HALF + h * 128 : HALF + (h + 1) * 128
            ]
    for h in range(OWN_HEADS):
        kh = k[h, 0:CHUNK, :]
        vh = v[h, 0:CHUNK, :]

        def step(dx, carry):
            acc_k, acc_v = carry
            xa = lax.rem(pos[1] + dx, 4)
            for dz in range(2):
                at = pl.multiple_of(dz * 1024 + dx * CHUNK, CHUNK)
                qc = q[h, pl.ds(at, CHUNK), :]
                dc = ds[h, pl.ds(at, CHUNK), :]
                log_total = stats[xa, h : h + 1, dz * CHUNK : (dz + 1) * CHUNK]
                delta = stats[xa, h + OWN_HEADS : h + OWN_HEADS + 1, dz * CHUNK : (dz + 1) * CHUNK]
                p = jnp.exp(nt(kh, qc) * SCALE - log_total)
                acc_v = acc_v + nn(p.astype(BF16), dc)
                dsc = (p * (nt(vh, dc) - delta)).astype(BF16)
                acc_k = acc_k + nn(dsc, qc)
            return acc_k, acc_v

        zero = jnp.zeros((CHUNK, HEAD_DIM), F32)
        acc_k, acc_v = lax.fori_loop(0, 4, step, (zero, zero))
        dk[h, :, :] = (acc_k * SCALE).astype(BF16)
        dv[h, :, :] = acc_v.astype(BF16)


def conv_body(mine, recv, w_own, w_oth, ext, gain, taps, gh, gc, usum, ns):
    g = gain[0:1, :]
    for r in range(0, 160, 16):
        ns[r : r + 16, :] = normalize(ext[r : r + 16, :].astype(F32))
    gh[...] = nt(mine[...], w_own[...]) + nt(recv[...], w_oth[...])
    for j in range(0, C, 128):
        tap = [taps[t : t + 1, j : j + 128] for t in range(5)]
        sums = [jnp.zeros((8, 128), F32) for _ in range(5)]
        gj = g[:, j : j + 128]
        for r in range(0, BLOCK, 64):
            near = [ns[14 + r + t : 78 + r + t, j : j + 128] for t in range(5)]
            u = tap[0] * (near[0] * gj)
            for t in range(1, 5):
                u = u + tap[t] * (near[t] * gj)
            inner = GELU_ROOT * (u + 0.044715 * u * u * u)
            th = jnp.tanh(inner)
            slope = 0.5 * (1.0 + th) + 0.5 * u * (1.0 - th * th) * GELU_ROOT * (
                1.0 + 3.0 * 0.044715 * u * u
            )
            gcv = gh[r : r + 64, j : j + 128] * slope
            gc[r : r + 64, j : j + 128] = gcv
            for t in range(5):
                sums[t] = sums[t] + jnp.sum((gcv * near[t]).reshape(8, 8, 128), axis=0)
        for t in range(5):
            usum[t : t + 1, j : j + 128] = jnp.sum(sums[t], axis=0, keepdims=True)
        usum[5:8, j : j + 128] = jnp.zeros((3, 128), F32)


def final_body(gh, gc, before, after, ext, gain, taps, out, es):
    es[0:8, :] = before[...]
    es[8:136, :] = gc[...]
    es[136:144, :] = after[...]
    g = gain[0:1, :]
    tap = [taps[t : t + 1, :] for t in range(5)]
    for r in range(0, BLOCK, 16):
        gn = tap[0] * es[10 + r : 26 + r, :]
        for t in range(1, 5):
            gn = gn + tap[t] * es[10 + r - t : 26 + r - t, :]
        x = ext[16 + r : 32 + r, :].astype(F32)
        inv = lax.rsqrt(jnp.mean(x * x, axis=-1, keepdims=True) + EPSILON)
        scaled = gn * g
        inner = jnp.mean(scaled * x, axis=-1, keepdims=True)
        res = gh[r : r + 16, :] + inv * scaled - x * (inv * inv * inv * inner)
        out[r : r + 16, :] = res.astype(BF16)


AXES = ("y", "zm", "zl", "zh", "x", "core")


def swap(a, axis):
    return lax.ppermute(a, axis, [(0, 1), (1, 0)])


def from_x(a, step):
    return lax.ppermute(a, "x", [((i + step) % 4, i) for i in range(4)])


def share(a, axes, size):
    wide = jnp.broadcast_to(a[None], (size,) + a.shape)
    return lax.all_to_all(wide, axes, 0, 0)


def shards(signal, norm_gain, conv_taps, w_query, w_key, w_value, cotangent):
    zh = lax.axis_index("zh")
    xi = lax.axis_index("x")
    core = lax.axis_index("core")
    pos = jnp.stack([zh, xi, core]).astype(jnp.int32)
    first = core == 0
    sig = signal[0]
    cot = cotangent[0]
    gain = norm_gain.reshape(1, C)

    def halves(a):
        low, high = a[:, :HALF], a[:, HALF:]
        return jnp.where(first, low, high), jnp.where(first, high, low)

    sig_z = swap(sig, "zh")
    keep, give = halves(cot)
    got = swap(give, "core")
    cot_own = jnp.concatenate(
        [jnp.where(first, keep, got), jnp.where(first, got, keep)], axis=1
    )
    cot_z = swap(cot_own, "zh")
    both = jnp.concatenate([sig, cot_own], axis=0)
    near = [from_x(both, d) for d in (1, 2, 3)]
    far = [from_x(sig_z, d) for d in (1, 2, 3)]
    e0 = swap(jnp.concatenate([sig] + [n[:BLOCK] for n in near], axis=0), "core")
    e1 = swap(jnp.concatenate([sig_z] + far, axis=0), "core")
    cot_far = [from_x(cot_z, d) for d in (1, 2, 3)]

    parts = [halves(w) for w in (w_query, w_key, w_value)]
    w_own = jnp.concatenate([p[0] for p in parts], axis=1)
    w_oth = jnp.concatenate([p[1] for p in parts], axis=1)

    head_shape = jax.ShapeDtypeStruct((OWN_HEADS, BINS, HEAD_DIM), BF16)
    q, k, v, ext = call(
        hidden_body,
        (head_shape, head_shape, head_shape, jax.ShapeDtypeStruct((160, C), BF16)),
        (pos, sig, *near, sig_z, *far, e0, e1, w_own, gain, conv_taps),
        (VM((CHUNKS, CHUNK, C), BF16), VM((288, C), F32), VM((CHUNK, C), BF16)),
    )
    part = jax.ShapeDtypeStruct((OWN_HEADS, CHUNK, HEAD_DIM), BF16)
    dq, stats = call(
        forward_body,
        (part, jax.ShapeDtypeStruct((8, 2 * CHUNK), F32)),
        (q, k, v, cot_own, cot_z),
        (
            VM((OWN_HEADS, 2 * CHUNK, HEAD_DIM), BF16),
            VM((CHUNK, BINS), F32),
            VM((2 * CHUNK, 128), F32),
        ),
    )
    stats_all = share(stats, "x", 4)
    dk, dv = call(
        backward_body,
        (part, part),
        (pos, q, k, v, cot_own, *near, cot_z, *cot_far, stats_all),
        (VM((OWN_HEADS, BINS, HEAD_DIM), BF16),),
    )
    grads = jnp.concatenate([dq[h] for h in range(3)] + [dk[h] for h in range(3)] + [dv[h] for h in range(3)], axis=1)
    mine = jnp.where(first, grads[:BLOCK], grads[BLOCK:])
    give = jnp.where(first, grads[BLOCK:], grads[:BLOCK])
    recv = swap(give, "core")
    wide = jax.ShapeDtypeStruct((BLOCK, C), F32)
    gh, gc, usum = call(
        conv_body,
        (wide, wide, jax.ShapeDtypeStruct((8, C), F32)),
        (mine, recv, w_own, w_oth, ext, gain, conv_taps),
        (VM((160, C), F32),),
    )
    ring = ("zh", "x", "core")
    before = lax.ppermute(gc[BLOCK - 8 :], ring, [(i, i + 1) for i in range(15)])
    after = lax.ppermute(gc[:8], ring, [(i + 1, i) for i in range(15)])
    out = call(
        final_body,
        jax.ShapeDtypeStruct((BLOCK, C), BF16),
        (gh, gc, before, after, ext, gain, conv_taps),
        (VM((144, C), F32),),
    )
    usum = usum + swap(usum, "core")
    usum = jnp.sum(share(usum, ("y", "x"), 16), axis=0)
    usum = jnp.sum(share(usum, ("zl",), 4), axis=0)
    usum = jnp.sum(share(usum, ("zm", "zh"), 4), axis=0)[:5]
    grad_taps = usum * gain
    grad_gain = jnp.sum(usum * conv_taps, axis=0)
    return out[None], grad_taps, grad_gain


def solution(mesh):
    shape = (mesh.devices.size // 128, 2, 4, 2, 4, 2)
    fine = Mesh(mesh.devices.reshape(shape), AXES)
    rows = P(("y", "zm", "zl"), ("zh", "x", "core"), None)
    in_specs = (rows, P(), P(), P(), P(), P(), rows)
    out_specs = (rows, P(), P())
    return jax.shard_map(shards, mesh=fine, in_specs=in_specs, out_specs=out_specs, check_vma=False)
```

```python
import math

import jax
import jax.numpy as jnp
from jax import lax
from jax.experimental import pallas as pl
from jax.experimental.pallas import tpu as pltpu
from jax.sharding import Mesh
from jax.sharding import PartitionSpec as P

HEADS = 6
HEAD_DIM = 128
OWN_HEADS = 3
HALF = OWN_HEADS * HEAD_DIM
EPSILON = 1e-06
GELU_ROOT = math.sqrt(2.0 / math.pi)
SCALE = 1.0 / math.sqrt(HEAD_DIM)
BLOCK = 128
CHUNK = 256
CHUNKS = 8
BINS = 2048
C = 768
INTERPRET = False
F32 = jnp.float32
BF16 = jnp.bfloat16
VM = pltpu.VMEM


def vspec():
    return pl.BlockSpec(memory_space=pltpu.VMEM)


def sspec():
    return pl.BlockSpec(memory_space=pltpu.SMEM)


def call(body, out_shape, args, scratch=(), limit=16):
    specs = [sspec() if a.dtype == jnp.int32 else vspec() for a in args]
    outs = jax.tree.map(lambda _: vspec(), out_shape)
    return pl.pallas_call(
        body,
        out_shape=out_shape,
        in_specs=specs,
        out_specs=outs,
        scratch_shapes=list(scratch),
        compiler_params=pltpu.CompilerParams(vmem_limit_bytes=limit << 20),
        interpret=INTERPRET,
    )(*args)


def nt(a, b):
    return lax.dot_general(a, b, (((1,), (1,)), ((), ())), preferred_element_type=F32)


def nn(a, b):
    return lax.dot_general(a, b, (((1,), (0,)), ((), ())), preferred_element_type=F32)


def neighbours(pos, dz, dx):
    zh = pos[0]
    xa = lax.rem(pos[1] + dx, 4)
    za = lax.rem(zh + dz, 2)
    wrap_lo = (xa == 0).astype(jnp.int32)
    wrap_hi = (xa == 3).astype(jnp.int32)
    prev = lax.rem(dz + wrap_lo, 2) * 4 + lax.rem(dx + 3, 4)
    nxt = lax.rem(dz + wrap_hi, 2) * 4 + lax.rem(dx + 1, 4)
    prev_ok = 1 - wrap_lo * (1 - za)
    nxt_ok = 1 - wrap_hi * za
    return prev, nxt, prev_ok.astype(F32), nxt_ok.astype(F32)


def normalize(rows):
    return rows * lax.rsqrt(jnp.mean(rows * rows, axis=-1, keepdims=True) + EPSILON)


def hidden_body(
    pos, c0, c1, e0, e1, w, gain, taps, q, k, v, ext, xs, ns, hs
):
    core = pos[2]
    here = pl.multiple_of(core * BLOCK, BLOCK)
    there = pl.multiple_of((1 - core) * BLOCK, BLOCK)
    for c in range(CHUNKS):
        own, other = ((c0, e0), (c1, e1))[c // 4]
        sl = slice((c % 4) * BLOCK, (c % 4 + 1) * BLOCK)
        xs[c, pl.ds(here, BLOCK), :] = own[sl, :]
        xs[c, pl.ds(there, BLOCK), :] = other[sl, :]
    prev, nxt, prev_ok, nxt_ok = neighbours(pos, jnp.int32(0), jnp.int32(0))
    first = core == 0
    ext[16:144, :] = c0[0:BLOCK, :]

    @pl.when(first)
    def _():
        ext[0:16, :] = (xs[prev, 240:256, :].astype(F32) * prev_ok).astype(BF16)
        ext[144:160, :] = xs[0, 128:144, :]

    @pl.when(jnp.logical_not(first))
    def _():
        ext[0:16, :] = xs[0, 112:128, :]
        ext[144:160, :] = (xs[nxt, 0:16, :].astype(F32) * nxt_ok).astype(BF16)

    def chunk(c, _):
        dz = lax.div(c, 4)
        dx = lax.rem(c, 4)
        prev, nxt, prev_ok, nxt_ok = neighbours(pos, dz, dx)
        g = gain[0:1, :]
        ns[0:16, :] = normalize(xs[prev, 240:256, :].astype(F32)) * g * prev_ok
        ns[272:288, :] = normalize(xs[nxt, 0:16, :].astype(F32)) * g * nxt_ok
        for r in range(0, CHUNK, 16):
            ns[16 + r : 32 + r, :] = normalize(xs[c, r : r + 16, :].astype(F32)) * g
        for j in range(0, C, 128):
            tap = [taps[t : t + 1, j : j + 128] for t in range(5)]
            for r in range(0, CHUNK, 64):
                u = tap[0] * ns[14 + r : 78 + r, j : j + 128]
                for t in range(1, 5):
                    u = u + tap[t] * ns[14 + r + t : 78 + r + t, j : j + 128]
                inner = GELU_ROOT * (u + 0.044715 * u * u * u)
                act = 0.5 * u * (1.0 + jnp.tanh(inner))
                x = xs[c, r : r + 64, j : j + 128].astype(F32)
                hs[r : r + 64, j : j + 128] = (x + act).astype(BF16)
        y = nn(hs[...], w[...]).astype(BF16)
        at = pl.multiple_of(c * CHUNK, CHUNK)
        for h in range(OWN_HEADS):
            q[h, pl.ds(at, CHUNK), :] = y[:, h * 128 : (h + 1) * 128]
            k[h, pl.ds(at, CHUNK), :] = y[:, HALF + h * 128 : HALF + (h + 1) * 128]
            v[h, pl.ds(at, CHUNK), :] = y[:, 2 * HALF + h * 128 : 2 * HALF + (h + 1) * 128]
        return 0

    lax.fori_loop(0, CHUNKS, chunk, 0)


KB = 512


def forward_body(q, k, v, d0, d4, dq, stats, ds, ss, sm):
    for g, d in enumerate((d0, d4)):
        for h in range(OWN_HEADS):
            ds[h, g * CHUNK : g * CHUNK + BLOCK, :] = d[0:BLOCK, h * 128 : (h + 1) * 128]
            ds[h, g * CHUNK + BLOCK : (g + 1) * CHUNK, :] = d[
                0:BLOCK, HALF + h * 128 : HALF + (h + 1) * 128
            ]
    sm[...] = jnp.zeros_like(sm)
    lane = lax.broadcasted_iota(jnp.int32, (CHUNK, 128), 1)

    def head(h, _):
        for g in range(2):
            qh = q[h, g * 1024 : g * 1024 + CHUNK, :]
            top = None
            for b in range(0, BINS, KB):
                s = nt(qh, k[h, b : b + KB, :])
                ss[:, b : b + KB] = s
                m = jnp.max(s, axis=1, keepdims=True)
                top = m if top is None else jnp.maximum(top, m)
            total = jnp.zeros((CHUNK, 1), F32)
            out = jnp.zeros((CHUNK, HEAD_DIM), F32)
            for b in range(0, BINS, KB):
                p = jnp.exp((ss[:, b : b + KB] - top) * SCALE)
                total = total + jnp.sum(p, axis=1, keepdims=True)
                out = out + nn(p.astype(BF16), v[h, b : b + KB, :])
                if g == 0:
                    ss[:, b : b + KB] = p
            inverse = 1.0 / total
            attended = (out * inverse).astype(BF16).astype(F32)
            do = ds[h, g * CHUNK : (g + 1) * CHUNK, :]
            delta = jnp.sum(do.astype(F32) * attended, axis=1, keepdims=True)
            log_total = top * SCALE + jnp.log(total)
            sl = slice(g * CHUNK, (g + 1) * CHUNK)
            sm[sl, :] = jnp.where(
                lane == h, log_total, jnp.where(lane == h + OWN_HEADS, delta, sm[sl, :])
            )
            if g == 0:
                acc = jnp.zeros((CHUNK, HEAD_DIM), F32)
                for b in range(0, BINS, KB):
                    dp = nt(do, v[h, b : b + KB, :])
                    dsc = (ss[:, b : b + KB] * inverse * (dp - delta)).astype(BF16)
                    acc = acc + nn(dsc, k[h, b : b + KB, :])
                dq[h, :, :] = (acc * SCALE).astype(BF16)
        return 0

    lax.fori_loop(0, OWN_HEADS, head, 0)
    stats[...] = jnp.transpose(sm[...])[0:8, :]


def backward_body(pos, q, k, v, dq, d0, d4, b1, b2, b3, stats, mine, give, ds, gs):
    core = pos[2]
    here = pl.multiple_of(core * BLOCK, BLOCK)
    there = pl.multiple_of((1 - core) * BLOCK, BLOCK)
    blocks = ((d0, 0), (b1, 0), (b2, 0), (b3, 0), (d4, 0), (b1, BLOCK), (b2, BLOCK), (b3, BLOCK))
    for c, (d, low) in enumerate(blocks):
        for h in range(OWN_HEADS):
            ds[h, c * CHUNK : c * CHUNK + BLOCK, :] = d[
                low : low + BLOCK, h * 128 : (h + 1) * 128
            ]
            ds[h, c * CHUNK + BLOCK : (c + 1) * CHUNK, :] = d[
                low : low + BLOCK, HALF + h * 128 : HALF + (h + 1) * 128
            ]
    for h in range(OWN_HEADS):
        kh = k[h, 0:CHUNK, :]
        vh = v[h, 0:CHUNK, :]

        def step(dx, carry):
            acc_k, acc_v = carry
            xa = lax.rem(pos[1] + dx, 4)
            for dz in range(2):
                at = pl.multiple_of(dz * 1024 + dx * CHUNK, CHUNK)
                qc = q[h, pl.ds(at, CHUNK), :]
                dc = ds[h, pl.ds(at, CHUNK), :]
                log_total = stats[xa, h : h + 1, dz * CHUNK : (dz + 1) * CHUNK]
                delta = stats[xa, h + OWN_HEADS : h + OWN_HEADS + 1, dz * CHUNK : (dz + 1) * CHUNK]
                p = jnp.exp(nt(kh, qc) * SCALE - log_total)
                acc_v = acc_v + nn(p.astype(BF16), dc)
                dsc = (p * (nt(vh, dc) - delta)).astype(BF16)
                acc_k = acc_k + nn(dsc, qc)
            return acc_k, acc_v

        zero = jnp.zeros((CHUNK, HEAD_DIM), F32)
        acc_k, acc_v = lax.fori_loop(0, 4, step, (zero, zero))
        gs[:, h * 128 : (h + 1) * 128] = dq[h]
        gs[:, HALF + h * 128 : HALF + (h + 1) * 128] = (acc_k * SCALE).astype(BF16)
        gs[:, 2 * HALF + h * 128 : 2 * HALF + (h + 1) * 128] = acc_v.astype(BF16)
    mine[...] = gs[pl.ds(here, BLOCK), :]
    give[...] = gs[pl.ds(there, BLOCK), :]


def conv_body(mine, recv, w_own, w_oth, ext, gain, taps, gh, gc, usum, ns):
    g = gain[0:1, :]
    for r in range(0, 160, 16):
        ns[r : r + 16, :] = normalize(ext[r : r + 16, :].astype(F32))
    gh[...] = nt(mine[...], w_own[...]) + nt(recv[...], w_oth[...])
    for j in range(0, C, 128):
        tap = [taps[t : t + 1, j : j + 128] for t in range(5)]
        sums = [jnp.zeros((8, 128), F32) for _ in range(5)]
        gj = g[:, j : j + 128]
        for r in range(0, BLOCK, 64):
            near = [ns[14 + r + t : 78 + r + t, j : j + 128] for t in range(5)]
            u = tap[0] * (near[0] * gj)
            for t in range(1, 5):
                u = u + tap[t] * (near[t] * gj)
            inner = GELU_ROOT * (u + 0.044715 * u * u * u)
            th = jnp.tanh(inner)
            slope = 0.5 * (1.0 + th) + 0.5 * u * (1.0 - th * th) * GELU_ROOT * (
                1.0 + 3.0 * 0.044715 * u * u
            )
            gcv = gh[r : r + 64, j : j + 128] * slope
            gc[r : r + 64, j : j + 128] = gcv
            for t in range(5):
                sums[t] = sums[t] + jnp.sum((gcv * near[t]).reshape(8, 8, 128), axis=0)
        side, slot = divmod(j // 128, OWN_HEADS)
        for t in range(5):
            row = t * OWN_HEADS + slot
            usum[side, row : row + 1, :] = jnp.sum(sums[t], axis=0, keepdims=True)
    usum[:, 15:16, :] = jnp.zeros((2, 1, 128), F32)


def final_body(gh, gc, before, after, ext, gain, taps, out, es):
    es[0:8, :] = before[...]
    es[8:136, :] = gc[...]
    es[136:144, :] = after[...]
    g = gain[0:1, :]
    tap = [taps[t : t + 1, :] for t in range(5)]
    for r in range(0, BLOCK, 16):
        gn = tap[0] * es[10 + r : 26 + r, :]
        for t in range(1, 5):
            gn = gn + tap[t] * es[10 + r - t : 26 + r - t, :]
        x = ext[16 + r : 32 + r, :].astype(F32)
        inv = lax.rsqrt(jnp.mean(x * x, axis=-1, keepdims=True) + EPSILON)
        scaled = gn * g
        inner = jnp.mean(scaled * x, axis=-1, keepdims=True)
        res = gh[r : r + 16, :] + inv * scaled - x * (inv * inv * inv * inner)
        out[r : r + 16, :] = res.astype(BF16)


AXES = ("y", "zm", "zl", "zh", "x", "core")


def swap(a, axis):
    return lax.ppermute(a, axis, [(0, 1), (1, 0)])


def from_x(a, step):
    return lax.ppermute(a, "x", [((i + step) % 4, i) for i in range(4)])


def share(a, axes, size):
    wide = jnp.broadcast_to(a[None], (size,) + a.shape)
    return lax.all_to_all(wide, axes, 0, 0)


def shards(signal, norm_gain, conv_taps, w_query, w_key, w_value, cotangent):
    zh = lax.axis_index("zh")
    xi = lax.axis_index("x")
    core = lax.axis_index("core")
    pos = jnp.stack([zh, xi, core]).astype(jnp.int32)
    first = core == 0
    sig = signal[0]
    cot = cotangent[0]
    gain = norm_gain.reshape(1, C)

    def halves(a):
        low, high = a[:, :HALF], a[:, HALF:]
        return jnp.where(first, low, high), jnp.where(first, high, low)

    keep, give = halves(cot)
    got = swap(give, "core")
    cot_own = jnp.concatenate(
        [jnp.where(first, keep, got), jnp.where(first, got, keep)], axis=1
    )
    sig_z = swap(sig, "zh")
    near = [from_x(sig, d) for d in (1, 2, 3)]
    sig_z, near = lax.optimization_barrier((sig_z, near))
    cot_z = swap(lax.optimization_barrier((cot_own, sig_z))[0], "zh")
    far = [from_x(sig_z, d) for d in (1, 2, 3)]
    c0 = jnp.concatenate([sig] + near, axis=0)
    e0 = swap(c0, "core")
    far, cot_z = lax.optimization_barrier((far, cot_z))
    c1 = jnp.concatenate([sig_z] + far, axis=0)
    e1 = swap(c1, "core")
    both = jnp.concatenate([cot_own, cot_z], axis=0)
    cots = [from_x(both, d) for d in (1, 2, 3)]

    parts = [halves(w) for w in (w_query, w_key, w_value)]
    w_own = jnp.concatenate([p[0] for p in parts], axis=1)
    w_oth = jnp.concatenate([p[1] for p in parts], axis=1)

    head_shape = jax.ShapeDtypeStruct((OWN_HEADS, BINS, HEAD_DIM), BF16)
    q, k, v, ext = call(
        hidden_body,
        (head_shape, head_shape, head_shape, jax.ShapeDtypeStruct((160, C), BF16)),
        (pos, c0, c1, e0, e1, w_own, gain, conv_taps),
        (VM((CHUNKS, CHUNK, C), BF16), VM((288, C), F32), VM((CHUNK, C), BF16)),
    )
    part = jax.ShapeDtypeStruct((OWN_HEADS, CHUNK, HEAD_DIM), BF16)
    dq, stats = call(
        forward_body,
        (part, jax.ShapeDtypeStruct((8, 2 * CHUNK), F32)),
        (q, k, v, cot_own, cot_z),
        (
            VM((OWN_HEADS, 2 * CHUNK, HEAD_DIM), BF16),
            VM((CHUNK, BINS), F32),
            VM((2 * CHUNK, 128), F32),
        ),
    )
    stats, cots = lax.optimization_barrier((stats, cots))
    stats_all = share(stats, "x", 4)
    grads = jax.ShapeDtypeStruct((BLOCK, 3 * HALF), BF16)
    mine, give = call(
        backward_body,
        (grads, grads),
        (pos, q, k, v, dq, cot_own, cot_z, *cots, stats_all),
        (VM((OWN_HEADS, BINS, HEAD_DIM), BF16), VM((CHUNK, 3 * HALF), BF16)),
    )
    recv = swap(give, "core")
    wide = jax.ShapeDtypeStruct((BLOCK, C), F32)
    gh, gc, usum = call(
        conv_body,
        (wide, wide, jax.ShapeDtypeStruct((2, 16, 128), F32)),
        (mine, recv, w_own, w_oth, ext, gain, conv_taps),
        (VM((160, C), F32),),
    )
    ring = ("zh", "x", "core")
    before = lax.ppermute(gc[BLOCK - 8 :], ring, [(i, i + 1) for i in range(15)])
    after = lax.ppermute(gc[:8], ring, [(i + 1, i) for i in range(15)])
    out = call(
        final_body,
        jax.ShapeDtypeStruct((BLOCK, C), BF16),
        (gh, gc, before, after, ext, gain, conv_taps),
        (VM((144, C), F32),),
    )
    wide = jnp.broadcast_to(usum[None], (16, 2, 16, 128)).reshape(32, 16, 128)
    part = jnp.sum(lax.all_to_all(wide, ("y", "x", "core"), 0, 0), axis=0)
    part = share(part.astype(BF16), ("zm", "zl", "zh"), 16).astype(F32)
    part = jnp.sum(part, axis=0)
    usum = lax.all_gather(part, "core", axis=0)[:, :15].reshape(2, 5, HALF)
    usum = jnp.concatenate([usum[0], usum[1]], axis=1)
    grad_taps = usum * gain
    grad_gain = jnp.sum(usum * conv_taps, axis=0)
    return out[None], grad_taps, grad_gain


def solution(mesh):
    shape = (mesh.devices.size // 128, 2, 4, 2, 4, 2)
    fine = Mesh(mesh.devices.reshape(shape), AXES)
    rows = P(("y", "zm", "zl"), ("zh", "x", "core"), None)
    in_specs = (rows, P(), P(), P(), P(), P(), rows)
    out_specs = (rows, P(), P())
    return jax.shard_map(shards, mesh=fine, in_specs=in_specs, out_specs=out_specs, check_vma=False)
```

```python
import math

import jax
import jax.numpy as jnp
from jax import lax
from jax.experimental import pallas as pl
from jax.experimental.pallas import tpu as pltpu
from jax.sharding import Mesh
from jax.sharding import PartitionSpec as P

HEADS = 6
HEAD_DIM = 128
OWN_HEADS = 3
HALF = OWN_HEADS * HEAD_DIM
EPSILON = 1e-06
GELU_ROOT = math.sqrt(2.0 / math.pi)
SCALE = 1.0 / math.sqrt(HEAD_DIM)
BLOCK = 128
CHUNK = 256
CHUNKS = 8
BINS = 2048
C = 768
INTERPRET = False
F32 = jnp.float32
BF16 = jnp.bfloat16
VM = pltpu.VMEM


def vspec():
    return pl.BlockSpec(memory_space=pltpu.VMEM)


def sspec():
    return pl.BlockSpec(memory_space=pltpu.SMEM)


def call(body, out_shape, args, scratch=(), limit=16):
    specs = [sspec() if a.dtype == jnp.int32 else vspec() for a in args]
    outs = jax.tree.map(lambda _: vspec(), out_shape)
    return pl.pallas_call(
        body,
        out_shape=out_shape,
        in_specs=specs,
        out_specs=outs,
        scratch_shapes=list(scratch),
        compiler_params=pltpu.CompilerParams(vmem_limit_bytes=limit << 20),
        interpret=INTERPRET,
    )(*args)


def nt(a, b):
    return lax.dot_general(a, b, (((1,), (1,)), ((), ())), preferred_element_type=F32)


def nn(a, b):
    return lax.dot_general(a, b, (((1,), (0,)), ((), ())), preferred_element_type=F32)


def neighbours(pos, dz, dx):
    zh = pos[0]
    xa = lax.rem(pos[1] + dx, 4)
    za = lax.rem(zh + dz, 2)
    wrap_lo = (xa == 0).astype(jnp.int32)
    wrap_hi = (xa == 3).astype(jnp.int32)
    prev = lax.rem(dz + wrap_lo, 2) * 4 + lax.rem(dx + 3, 4)
    nxt = lax.rem(dz + wrap_hi, 2) * 4 + lax.rem(dx + 1, 4)
    prev_ok = 1 - wrap_lo * (1 - za)
    nxt_ok = 1 - wrap_hi * za
    return prev, nxt, prev_ok.astype(F32), nxt_ok.astype(F32)


def normalize(rows):
    return rows * lax.rsqrt(jnp.mean(rows * rows, axis=-1, keepdims=True) + EPSILON)


def hidden_body(
    pos, near, other, w, gain, taps, q, k, v, ext, xs, ns, hs
):
    core = pos[2]
    here = pl.multiple_of(core * BLOCK, BLOCK)
    there = pl.multiple_of((1 - core) * BLOCK, BLOCK)
    for c in range(CHUNKS):
        xa = lax.rem(pos[1] + c % 4, 4)
        sl = slice((c // 4) * BLOCK, (c // 4 + 1) * BLOCK)
        xs[c, pl.ds(here, BLOCK), :] = near[xa, sl, :]
        xs[c, pl.ds(there, BLOCK), :] = other[xa, sl, :]
    prev, nxt, prev_ok, nxt_ok = neighbours(pos, jnp.int32(0), jnp.int32(0))
    first = core == 0
    ext[16:144, :] = near[pos[1], 0:BLOCK, :]

    @pl.when(first)
    def _():
        ext[0:16, :] = (xs[prev, 240:256, :].astype(F32) * prev_ok).astype(BF16)
        ext[144:160, :] = xs[0, 128:144, :]

    @pl.when(jnp.logical_not(first))
    def _():
        ext[0:16, :] = xs[0, 112:128, :]
        ext[144:160, :] = (xs[nxt, 0:16, :].astype(F32) * nxt_ok).astype(BF16)

    def chunk(c, _):
        dz = lax.div(c, 4)
        dx = lax.rem(c, 4)
        prev, nxt, prev_ok, nxt_ok = neighbours(pos, dz, dx)
        g = gain[0:1, :]
        ns[0:16, :] = normalize(xs[prev, 240:256, :].astype(F32)) * g * prev_ok
        ns[272:288, :] = normalize(xs[nxt, 0:16, :].astype(F32)) * g * nxt_ok
        for r in range(0, CHUNK, 16):
            ns[16 + r : 32 + r, :] = normalize(xs[c, r : r + 16, :].astype(F32)) * g
        for j in range(0, C, 128):
            tap = [taps[t : t + 1, j : j + 128] for t in range(5)]
            for r in range(0, CHUNK, 64):
                u = tap[0] * ns[14 + r : 78 + r, j : j + 128]
                for t in range(1, 5):
                    u = u + tap[t] * ns[14 + r + t : 78 + r + t, j : j + 128]
                inner = GELU_ROOT * (u + 0.044715 * u * u * u)
                act = 0.5 * u * (1.0 + jnp.tanh(inner))
                x = xs[c, r : r + 64, j : j + 128].astype(F32)
                hs[r : r + 64, j : j + 128] = (x + act).astype(BF16)
        y = nn(hs[...], w[...]).astype(BF16)
        at = pl.multiple_of(c * CHUNK, CHUNK)
        for h in range(OWN_HEADS):
            q[h, pl.ds(at, CHUNK), :] = y[:, h * 128 : (h + 1) * 128]
            k[h, pl.ds(at, CHUNK), :] = y[:, HALF + h * 128 : HALF + (h + 1) * 128]
            v[h, pl.ds(at, CHUNK), :] = y[:, 2 * HALF + h * 128 : 2 * HALF + (h + 1) * 128]
        return 0

    lax.fori_loop(0, CHUNKS, chunk, 0)


KB = 512


def forward_body(q, k, v, d0, d4, dq, stats, ds, ss, sm):
    for g, d in enumerate((d0, d4)):
        for h in range(OWN_HEADS):
            ds[h, g * CHUNK : g * CHUNK + BLOCK, :] = d[0:BLOCK, h * 128 : (h + 1) * 128]
            ds[h, g * CHUNK + BLOCK : (g + 1) * CHUNK, :] = d[
                0:BLOCK, HALF + h * 128 : HALF + (h + 1) * 128
            ]
    sm[...] = jnp.zeros_like(sm)
    lane = lax.broadcasted_iota(jnp.int32, (CHUNK, 128), 1)

    def head(h, _):
        for g in range(2):
            qh = q[h, g * 1024 : g * 1024 + CHUNK, :]
            top = None
            for b in range(0, BINS, KB):
                s = nt(qh, k[h, b : b + KB, :])
                ss[:, b : b + KB] = s
                m = jnp.max(s, axis=1, keepdims=True)
                top = m if top is None else jnp.maximum(top, m)
            total = jnp.zeros((CHUNK, 1), F32)
            out = jnp.zeros((CHUNK, HEAD_DIM), F32)
            for b in range(0, BINS, KB):
                p = jnp.exp((ss[:, b : b + KB] - top) * SCALE)
                total = total + jnp.sum(p, axis=1, keepdims=True)
                out = out + nn(p.astype(BF16), v[h, b : b + KB, :])
                if g == 0:
                    ss[:, b : b + KB] = p
            inverse = 1.0 / total
            attended = (out * inverse).astype(BF16).astype(F32)
            do = ds[h, g * CHUNK : (g + 1) * CHUNK, :]
            delta = jnp.sum(do.astype(F32) * attended, axis=1, keepdims=True)
            log_total = top * SCALE + jnp.log(total)
            sl = slice(g * CHUNK, (g + 1) * CHUNK)
            sm[sl, :] = jnp.where(
                lane == h, log_total, jnp.where(lane == h + OWN_HEADS, delta, sm[sl, :])
            )
            if g == 0:
                acc = jnp.zeros((CHUNK, HEAD_DIM), F32)
                for b in range(0, BINS, KB):
                    dp = nt(do, v[h, b : b + KB, :])
                    dsc = (ss[:, b : b + KB] * inverse * (dp - delta)).astype(BF16)
                    acc = acc + nn(dsc, k[h, b : b + KB, :])
                dq[h, :, :] = (acc * SCALE).astype(BF16)
        return 0

    lax.fori_loop(0, OWN_HEADS, head, 0)
    stats[...] = jnp.transpose(sm[...])[0:8, :]


def backward_body(pos, q, k, v, dq, d0, d4, b1, b2, b3, stats, mine, give, ds, gs):
    core = pos[2]
    here = pl.multiple_of(core * BLOCK, BLOCK)
    there = pl.multiple_of((1 - core) * BLOCK, BLOCK)
    blocks = ((d0, 0), (b1, 0), (b2, 0), (b3, 0), (d4, 0), (b1, BLOCK), (b2, BLOCK), (b3, BLOCK))
    for c, (d, low) in enumerate(blocks):
        for h in range(OWN_HEADS):
            ds[h, c * CHUNK : c * CHUNK + BLOCK, :] = d[
                low : low + BLOCK, h * 128 : (h + 1) * 128
            ]
            ds[h, c * CHUNK + BLOCK : (c + 1) * CHUNK, :] = d[
                low : low + BLOCK, HALF + h * 128 : HALF + (h + 1) * 128
            ]
    for h in range(OWN_HEADS):
        kh = k[h, 0:CHUNK, :]
        vh = v[h, 0:CHUNK, :]

        def step(dx, carry):
            acc_k, acc_v = carry
            xa = lax.rem(pos[1] + dx, 4)
            for dz in range(2):
                at = pl.multiple_of(dz * 1024 + dx * CHUNK, CHUNK)
                qc = q[h, pl.ds(at, CHUNK), :]
                dc = ds[h, pl.ds(at, CHUNK), :]
                log_total = stats[xa, h : h + 1, dz * CHUNK : (dz + 1) * CHUNK]
                delta = stats[xa, h + OWN_HEADS : h + OWN_HEADS + 1, dz * CHUNK : (dz + 1) * CHUNK]
                p = jnp.exp(nt(kh, qc) * SCALE - log_total)
                acc_v = acc_v + nn(p.astype(BF16), dc)
                dsc = (p * (nt(vh, dc) - delta)).astype(BF16)
                acc_k = acc_k + nn(dsc, qc)
            return acc_k, acc_v

        zero = jnp.zeros((CHUNK, HEAD_DIM), F32)
        acc_k, acc_v = lax.fori_loop(0, 4, step, (zero, zero))
        gs[:, h * 128 : (h + 1) * 128] = dq[h]
        gs[:, HALF + h * 128 : HALF + (h + 1) * 128] = (acc_k * SCALE).astype(BF16)
        gs[:, 2 * HALF + h * 128 : 2 * HALF + (h + 1) * 128] = acc_v.astype(BF16)
    mine[...] = gs[pl.ds(here, BLOCK), :]
    give[...] = gs[pl.ds(there, BLOCK), :]


def conv_body(pos, mine, recv, w_own, w_oth, ext, gain, taps, gh, gc, usum, inner_edge, outer_edge, ns):
    g = gain[0:1, :]
    for r in range(0, 160, 16):
        ns[r : r + 16, :] = normalize(ext[r : r + 16, :].astype(F32))
    gh[...] = nt(mine[...], w_own[...]) + nt(recv[...], w_oth[...])
    for j in range(0, C, 128):
        tap = [taps[t : t + 1, j : j + 128] for t in range(5)]
        sums = [jnp.zeros((8, 128), F32) for _ in range(5)]
        gj = g[:, j : j + 128]
        for r in range(0, BLOCK, 64):
            near = [ns[14 + r + t : 78 + r + t, j : j + 128] for t in range(5)]
            u = tap[0] * (near[0] * gj)
            for t in range(1, 5):
                u = u + tap[t] * (near[t] * gj)
            inner = GELU_ROOT * (u + 0.044715 * u * u * u)
            th = jnp.tanh(inner)
            slope = 0.5 * (1.0 + th) + 0.5 * u * (1.0 - th * th) * GELU_ROOT * (
                1.0 + 3.0 * 0.044715 * u * u
            )
            gcv = gh[r : r + 64, j : j + 128] * slope
            gc[r : r + 64, j : j + 128] = gcv
            for t in range(5):
                sums[t] = sums[t] + jnp.sum((gcv * near[t]).reshape(8, 8, 128), axis=0)
        side, slot = divmod(j // 128, OWN_HEADS)
        for t in range(5):
            row = t * OWN_HEADS + slot
            usum[side, row : row + 1, :] = jnp.sum(sums[t], axis=0, keepdims=True)
    usum[:, 15:16, :] = jnp.zeros((2, 1, 128), F32)
    first = pos[2] == 0
    head, tail = gc[0:8, :], gc[BLOCK - 8 : BLOCK, :]
    inner_edge[...] = jnp.where(first, tail, head)
    outer_edge[...] = jnp.where(first, head, tail)


def final_body(pos, gh, gc, inside, outside, ext, gain, taps, out, es):
    first = pos[2] == 0
    es[0:8, :] = jnp.where(first, outside[...], inside[...])
    es[8:136, :] = gc[...]
    es[136:144, :] = jnp.where(first, inside[...], outside[...])
    g = gain[0:1, :]
    tap = [taps[t : t + 1, :] for t in range(5)]
    for r in range(0, BLOCK, 16):
        gn = tap[0] * es[10 + r : 26 + r, :]
        for t in range(1, 5):
            gn = gn + tap[t] * es[10 + r - t : 26 + r - t, :]
        x = ext[16 + r : 32 + r, :].astype(F32)
        inv = lax.rsqrt(jnp.mean(x * x, axis=-1, keepdims=True) + EPSILON)
        scaled = gn * g
        inner = jnp.mean(scaled * x, axis=-1, keepdims=True)
        res = gh[r : r + 16, :] + inv * scaled - x * (inv * inv * inv * inner)
        out[r : r + 16, :] = res.astype(BF16)


AXES = ("y", "zm", "zl", "zh", "x", "core")


def swap(a, axis):
    return lax.ppermute(a, axis, [(0, 1), (1, 0)])


def from_x(a, step):
    return lax.ppermute(a, "x", [((i + step) % 4, i) for i in range(4)])


def share(a, axes, size):
    wide = jnp.broadcast_to(a[None], (size,) + a.shape)
    return lax.all_to_all(wide, axes, 0, 0)


def shards(signal, norm_gain, conv_taps, w_query, w_key, w_value, cotangent):
    zh = lax.axis_index("zh")
    xi = lax.axis_index("x")
    core = lax.axis_index("core")
    pos = jnp.stack([zh, xi, core]).astype(jnp.int32)
    first = core == 0
    sig = signal[0]
    cot = cotangent[0]
    gain = norm_gain.reshape(1, C)

    def halves(a):
        low, high = a[:, :HALF], a[:, HALF:]
        return jnp.where(first, low, high), jnp.where(first, high, low)

    keep, give = halves(cot)
    got = swap(give, "core")
    cot_own = jnp.concatenate(
        [jnp.where(first, keep, got), jnp.where(first, got, keep)], axis=1
    )
    sig_z = swap(sig, "zh")
    parts = [halves(w) for w in (w_query, w_key, w_value)]
    w_own = jnp.concatenate([p[0] for p in parts], axis=1)
    w_oth = jnp.concatenate([p[1] for p in parts], axis=1)
    sig_z, cot_own, w_own, w_oth = lax.optimization_barrier((sig_z, cot_own, w_own, w_oth))
    cot_z = swap(cot_own, "zh")
    near = share(jnp.concatenate([sig, sig_z], axis=0), "x", 4)
    other = swap(near, "core")

    head_shape = jax.ShapeDtypeStruct((OWN_HEADS, BINS, HEAD_DIM), BF16)
    q, k, v, ext = call(
        hidden_body,
        (head_shape, head_shape, head_shape, jax.ShapeDtypeStruct((160, C), BF16)),
        (pos, near, other, w_own, gain, conv_taps),
        (VM((CHUNKS, CHUNK, C), BF16), VM((288, C), F32), VM((CHUNK, C), BF16)),
    )
    cot_z, q = lax.optimization_barrier((cot_z, q))
    both = jnp.concatenate([cot_own, cot_z], axis=0)
    cots = [from_x(both, d) for d in (1, 2, 3)]
    part = jax.ShapeDtypeStruct((OWN_HEADS, CHUNK, HEAD_DIM), BF16)
    dq, stats = call(
        forward_body,
        (part, jax.ShapeDtypeStruct((8, 2 * CHUNK), F32)),
        (q, k, v, cot_own, cot_z),
        (
            VM((OWN_HEADS, 2 * CHUNK, HEAD_DIM), BF16),
            VM((CHUNK, BINS), F32),
            VM((2 * CHUNK, 128), F32),
        ),
    )
    stats, cots = lax.optimization_barrier((stats, cots))
    stats_all = share(stats, "x", 4)
    grads = jax.ShapeDtypeStruct((BLOCK, 3 * HALF), BF16)
    mine, give = call(
        backward_body,
        (grads, grads),
        (pos, q, k, v, dq, cot_own, cot_z, *cots, stats_all),
        (VM((OWN_HEADS, BINS, HEAD_DIM), BF16), VM((CHUNK, 3 * HALF), BF16)),
    )
    recv = swap(give, "core")
    wide = jax.ShapeDtypeStruct((BLOCK, C), F32)
    edge = jax.ShapeDtypeStruct((8, C), F32)
    gh, gc, usum, inside, outside = call(
        conv_body,
        (wide, wide, jax.ShapeDtypeStruct((2, 16, 128), F32), edge, edge),
        (pos, mine, recv, w_own, w_oth, ext, gain, conv_taps),
        (VM((160, C), F32),),
    )
    inside = swap(inside, "core")
    pairs = [(i, i + 1) for i in range(1, 15, 2)] + [(i + 1, i) for i in range(1, 15, 2)]
    outside = lax.ppermute(outside, ("zh", "x", "core"), pairs)
    out = call(
        final_body,
        jax.ShapeDtypeStruct((BLOCK, C), BF16),
        (pos, gh, gc, inside, outside, ext, gain, conv_taps),
        (VM((144, C), F32),),
    )
    wide = jnp.broadcast_to(usum[None], (16, 2, 16, 128)).reshape(32, 16, 128)
    part = jnp.sum(lax.all_to_all(wide, ("y", "x", "core"), 0, 0), axis=0)
    part = share(part.astype(BF16), ("zm", "zl", "zh"), 16).astype(F32)
    part = jnp.sum(part, axis=0)
    usum = lax.all_gather(part, "core", axis=0)[:, :15].reshape(2, 5, HALF)
    usum = jnp.concatenate([usum[0], usum[1]], axis=1)
    grad_taps = usum * gain
    grad_gain = jnp.sum(usum * conv_taps, axis=0)
    return out[None], grad_taps, grad_gain


def solution(mesh):
    shape = (mesh.devices.size // 128, 2, 4, 2, 4, 2)
    fine = Mesh(mesh.devices.reshape(shape), AXES)
    rows = P(("y", "zm", "zl"), ("zh", "x", "core"), None)
    in_specs = (rows, P(), P(), P(), P(), P(), rows)
    out_specs = (rows, P(), P())
    return jax.shard_map(shards, mesh=fine, in_specs=in_specs, out_specs=out_specs, check_vma=False)
```

```python
import math

import jax
import jax.numpy as jnp
from jax import lax
from jax.experimental import pallas as pl
from jax.experimental.pallas import tpu as pltpu
from jax.sharding import Mesh
from jax.sharding import PartitionSpec as P

HEADS = 6
HEAD_DIM = 128
OWN_HEADS = 3
HALF = OWN_HEADS * HEAD_DIM
EPSILON = 1e-06
GELU_ROOT = math.sqrt(2.0 / math.pi)
SCALE = 1.0 / math.sqrt(HEAD_DIM)
BLOCK = 128
CHUNK = 256
CHUNKS = 8
BINS = 2048
C = 768
INTERPRET = False
F32 = jnp.float32
BF16 = jnp.bfloat16
VM = pltpu.VMEM


def vspec():
    return pl.BlockSpec(memory_space=pltpu.VMEM)


def sspec():
    return pl.BlockSpec(memory_space=pltpu.SMEM)


def call(body, out_shape, args, scratch=(), limit=16):
    specs = [sspec() if a.dtype == jnp.int32 else vspec() for a in args]
    outs = jax.tree.map(lambda _: vspec(), out_shape)
    return pl.pallas_call(
        body,
        out_shape=out_shape,
        in_specs=specs,
        out_specs=outs,
        scratch_shapes=list(scratch),
        compiler_params=pltpu.CompilerParams(vmem_limit_bytes=limit << 20),
        interpret=INTERPRET,
    )(*args)


def nt(a, b):
    return lax.dot_general(a, b, (((1,), (1,)), ((), ())), preferred_element_type=F32)


def nn(a, b):
    return lax.dot_general(a, b, (((1,), (0,)), ((), ())), preferred_element_type=F32)


def neighbours(pos, dz, dx):
    zh = pos[0]
    xa = lax.rem(pos[1] + dx, 4)
    za = lax.rem(zh + dz, 2)
    wrap_lo = (xa == 0).astype(jnp.int32)
    wrap_hi = (xa == 3).astype(jnp.int32)
    prev = lax.rem(dz + wrap_lo, 2) * 4 + lax.rem(dx + 3, 4)
    nxt = lax.rem(dz + wrap_hi, 2) * 4 + lax.rem(dx + 1, 4)
    prev_ok = 1 - wrap_lo * (1 - za)
    nxt_ok = 1 - wrap_hi * za
    return prev, nxt, prev_ok.astype(F32), nxt_ok.astype(F32)


def normalize(rows):
    return rows * lax.rsqrt(jnp.mean(rows * rows, axis=-1, keepdims=True) + EPSILON)


def hidden_body(
    pos, near, other, w, gain, taps, q, k, v, ext, xs, ns, hs
):
    core = pos[2]
    here = pl.multiple_of(core * BLOCK, BLOCK)
    there = pl.multiple_of((1 - core) * BLOCK, BLOCK)
    for c in range(CHUNKS):
        xa = lax.rem(pos[1] + c % 4, 4)
        sl = slice((c // 4) * BLOCK, (c // 4 + 1) * BLOCK)
        xs[c, pl.ds(here, BLOCK), :] = near[xa, sl, :]
        xs[c, pl.ds(there, BLOCK), :] = other[xa, sl, :]
    prev, nxt, prev_ok, nxt_ok = neighbours(pos, jnp.int32(0), jnp.int32(0))
    first = core == 0
    ext[16:144, :] = near[pos[1], 0:BLOCK, :]

    @pl.when(first)
    def _():
        ext[0:16, :] = (xs[prev, 240:256, :].astype(F32) * prev_ok).astype(BF16)
        ext[144:160, :] = xs[0, 128:144, :]

    @pl.when(jnp.logical_not(first))
    def _():
        ext[0:16, :] = xs[0, 112:128, :]
        ext[144:160, :] = (xs[nxt, 0:16, :].astype(F32) * nxt_ok).astype(BF16)

    def chunk(c, _):
        dz = lax.div(c, 4)
        dx = lax.rem(c, 4)
        prev, nxt, prev_ok, nxt_ok = neighbours(pos, dz, dx)
        g = gain[0:1, :]
        ns[0:16, :] = normalize(xs[prev, 240:256, :].astype(F32)) * g * prev_ok
        ns[272:288, :] = normalize(xs[nxt, 0:16, :].astype(F32)) * g * nxt_ok
        for r in range(0, CHUNK, 16):
            ns[16 + r : 32 + r, :] = normalize(xs[c, r : r + 16, :].astype(F32)) * g
        for j in range(0, C, 128):
            tap = [taps[t : t + 1, j : j + 128] for t in range(5)]
            for r in range(0, CHUNK, 64):
                u = tap[0] * ns[14 + r : 78 + r, j : j + 128]
                for t in range(1, 5):
                    u = u + tap[t] * ns[14 + r + t : 78 + r + t, j : j + 128]
                inner = GELU_ROOT * (u + 0.044715 * u * u * u)
                act = 0.5 * u * (1.0 + jnp.tanh(inner))
                x = xs[c, r : r + 64, j : j + 128].astype(F32)
                hs[r : r + 64, j : j + 128] = (x + act).astype(BF16)
        y = nn(hs[...], w[...]).astype(BF16)
        at = pl.multiple_of(c * CHUNK, CHUNK)
        for h in range(OWN_HEADS):
            q[h, pl.ds(at, CHUNK), :] = y[:, h * 128 : (h + 1) * 128]
            k[h, pl.ds(at, CHUNK), :] = y[:, HALF + h * 128 : HALF + (h + 1) * 128]
            v[h, pl.ds(at, CHUNK), :] = y[:, 2 * HALF + h * 128 : 2 * HALF + (h + 1) * 128]
        return 0

    lax.fori_loop(0, CHUNKS, chunk, 0)


KB = 512


def forward_body(q, k, v, d, dq, stats, ds, ss, sm):
    for h in range(OWN_HEADS):
        ds[h, 0:BLOCK, :] = d[:, h * 128 : (h + 1) * 128]
        ds[h, BLOCK:CHUNK, :] = d[:, HALF + h * 128 : HALF + (h + 1) * 128]
    sm[...] = jnp.zeros_like(sm)
    lane = lax.broadcasted_iota(jnp.int32, (CHUNK, 128), 1)

    def head(h, _):
        qh = q[h, 0:CHUNK, :]
        top = None
        for b in range(0, BINS, KB):
            s = nt(qh, k[h, b : b + KB, :])
            ss[:, b : b + KB] = s
            m = jnp.max(s, axis=1, keepdims=True)
            top = m if top is None else jnp.maximum(top, m)
        total = jnp.zeros((CHUNK, 1), F32)
        out = jnp.zeros((CHUNK, HEAD_DIM), F32)
        for b in range(0, BINS, KB):
            p = jnp.exp((ss[:, b : b + KB] - top) * SCALE)
            total = total + jnp.sum(p, axis=1, keepdims=True)
            out = out + nn(p.astype(BF16), v[h, b : b + KB, :])
            ss[:, b : b + KB] = p
        inverse = 1.0 / total
        attended = (out * inverse).astype(BF16).astype(F32)
        do = ds[h]
        delta = jnp.sum(do.astype(F32) * attended, axis=1, keepdims=True)
        log_total = top * SCALE + jnp.log(total)
        sm[...] = jnp.where(lane == h, log_total, jnp.where(lane == h + OWN_HEADS, delta, sm[...]))
        acc = jnp.zeros((CHUNK, HEAD_DIM), F32)
        for b in range(0, BINS, KB):
            dp = nt(do, v[h, b : b + KB, :])
            dsc = (ss[:, b : b + KB] * inverse * (dp - delta)).astype(BF16)
            acc = acc + nn(dsc, k[h, b : b + KB, :])
        dq[h, :, :] = (acc * SCALE).astype(BF16)
        return 0

    lax.fori_loop(0, OWN_HEADS, head, 0)
    stats[...] = jnp.transpose(sm[...])[0:8, :]


EDGE = 16
WIDE = CHUNK + 2 * EDGE
WINDOW = BLOCK + 2 * EDGE


def backward_body(pos, q, k, v, dq, cots, stats, mine, give, ds, gs, kx, vx, qx, dx_, st):
    core = pos[2]

    def place(c):
        return lax.rem(pos[0] + lax.div(c, 4), 2) * 4 + lax.rem(pos[1] + c, 4)

    for c in range(CHUNKS):
        at = place(jnp.int32(c))
        for h in range(OWN_HEADS):
            lo = c * CHUNK
            ds[h, lo : lo + BLOCK, :] = cots[at, :, h * 128 : (h + 1) * 128]
            ds[h, lo + BLOCK : lo + CHUNK, :] = cots[at, :, HALF + h * 128 : HALF + (h + 1) * 128]
    prev, nxt, _, _ = neighbours(pos, jnp.int32(0), jnp.int32(0))
    low = pl.multiple_of(prev * CHUNK + CHUNK - EDGE, EDGE)
    high = pl.multiple_of(nxt * CHUNK, EDGE)
    for h in range(OWN_HEADS):
        for src, dst in ((k, kx), (v, vx)):
            dst[h, 0:EDGE, :] = src[h, pl.ds(low, EDGE), :]
            dst[h, EDGE : EDGE + CHUNK, :] = src[h, 0:CHUNK, :]
            dst[h, EDGE + CHUNK : WIDE, :] = src[h, pl.ds(high, EDGE), :]
        for src, dst in ((q, qx), (ds, dx_)):
            dst[h, 0:EDGE, :] = src[h, pl.ds(low, EDGE), :]
            dst[h, EDGE : 2 * EDGE, :] = src[h, pl.ds(high, EDGE), :]
    low_stats = jnp.transpose(jnp.tile(stats[place(prev), :, 128:256], (16, 1)))
    high_stats = jnp.transpose(jnp.tile(stats[place(nxt), :, 0:128], (16, 1)))
    st[0:EDGE, :] = low_stats[128 - EDGE : 128, :]
    st[EDGE : 2 * EDGE, :] = high_stats[0:EDGE, :]
    for h in range(OWN_HEADS):
        kh = kx[h]
        vh = vx[h]

        def step(dx, carry):
            acc_k, acc_v = carry
            for dz in range(2):
                c = dz * 4 + dx
                at = pl.multiple_of(c * CHUNK, CHUNK)
                qc = q[h, pl.ds(at, CHUNK), :]
                dc = ds[h, pl.ds(at, CHUNK), :]
                row = place(c)
                log_total = stats[row, h : h + 1, :]
                delta = stats[row, h + OWN_HEADS : h + OWN_HEADS + 1, :]
                p = jnp.exp(nt(kh, qc) * SCALE - log_total)
                acc_v = acc_v + nn(p.astype(BF16), dc)
                dsc = (p * (nt(vh, dc) - delta)).astype(BF16)
                acc_k = acc_k + nn(dsc, qc)
            return acc_k, acc_v

        zero = jnp.zeros((WIDE, HEAD_DIM), F32)
        acc_k, acc_v = lax.fori_loop(0, 4, step, (zero, zero))
        p = jnp.exp(nt(qx[h], k[h]) * SCALE - st[:, h : h + 1])
        dsc = (p * (nt(dx_[h], v[h]) - st[:, h + OWN_HEADS : h + OWN_HEADS + 1])).astype(BF16)
        dqx = (nn(dsc, k[h]) * SCALE).astype(BF16)
        cols = slice(h * 128, (h + 1) * 128)
        gs[0:EDGE, cols] = dqx[0:EDGE]
        gs[EDGE : EDGE + CHUNK, cols] = dq[h]
        gs[EDGE + CHUNK : WIDE, cols] = dqx[EDGE : 2 * EDGE]
        gs[:, HALF + h * 128 : HALF + (h + 1) * 128] = (acc_k * SCALE).astype(BF16)
        gs[:, 2 * HALF + h * 128 : 2 * HALF + (h + 1) * 128] = acc_v.astype(BF16)
    mine[...] = gs[pl.ds(pl.multiple_of(core * BLOCK, BLOCK), WINDOW), :]
    give[...] = gs[pl.ds(pl.multiple_of((1 - core) * BLOCK, BLOCK), WINDOW), :]


def conv_body(pos, mine, recv, w_own, w_oth, ext, gain, taps, out, usum, ns, gh, gc):
    _, _, prev_ok, nxt_ok = neighbours(pos, jnp.int32(0), jnp.int32(0))
    first = pos[2] == 0
    low_ok = jnp.where(first, prev_ok, 1.0)
    high_ok = jnp.where(first, 1.0, nxt_ok)
    g = gain[0:1, :]
    for r in range(0, WINDOW, 16):
        ns[r : r + 16, :] = normalize(ext[r : r + 16, :].astype(F32))
    gh[...] = nt(mine[...], w_own[...]) + nt(recv[...], w_oth[...])
    for j in range(0, C, 128):
        tap = [taps[t : t + 1, j : j + 128] for t in range(5)]
        gj = g[:, j : j + 128]
        cols = slice(j, j + 128)

        def grad(r, n):
            near = [ns[r - 2 + t : r - 2 + t + n, cols] for t in range(5)]
            u = tap[0] * (near[0] * gj)
            for t in range(1, 5):
                u = u + tap[t] * (near[t] * gj)
            inner = GELU_ROOT * (u + 0.044715 * u * u * u)
            th = jnp.tanh(inner)
            slope = 0.5 * (1.0 + th) + 0.5 * u * (1.0 - th * th) * GELU_ROOT * (
                1.0 + 3.0 * 0.044715 * u * u
            )
            return near, gh[r : r + n, cols] * slope

        _, edge = grad(8, 8)
        gc[8:16, cols] = edge * low_ok
        _, edge = grad(144, 8)
        gc[144:152, cols] = edge * high_ok
        sums = [jnp.zeros((8, 128), F32) for _ in range(5)]
        for r in range(EDGE, EDGE + BLOCK, 64):
            near, val = grad(r, 64)
            gc[r : r + 64, cols] = val
            for t in range(5):
                sums[t] = sums[t] + jnp.sum((val * near[t]).reshape(8, 8, 128), axis=0)
        side, slot = divmod(j // 128, OWN_HEADS)
        for t in range(5):
            row = t * OWN_HEADS + slot
            usum[side, row : row + 1, :] = jnp.sum(sums[t], axis=0, keepdims=True)
    usum[:, 15:16, :] = jnp.zeros((2, 1, 128), F32)
    tap = [taps[t : t + 1, :] for t in range(5)]
    for r in range(EDGE, EDGE + BLOCK, 16):
        gn = tap[0] * gc[r + 2 : r + 18, :]
        for t in range(1, 5):
            gn = gn + tap[t] * gc[r + 2 - t : r + 18 - t, :]
        x = ext[r : r + 16, :].astype(F32)
        inv = lax.rsqrt(jnp.mean(x * x, axis=-1, keepdims=True) + EPSILON)
        scaled = gn * g
        inner = jnp.mean(scaled * x, axis=-1, keepdims=True)
        res = gh[r : r + 16, :] + inv * scaled - x * (inv * inv * inv * inner)
        out[r - EDGE : r - EDGE + 16, :] = res.astype(BF16)


AXES = ("y", "zm", "zl", "zh", "x", "core")


def swap(a, axis):
    return lax.ppermute(a, axis, [(0, 1), (1, 0)])


def from_x(a, step):
    return lax.ppermute(a, "x", [((i + step) % 4, i) for i in range(4)])


def share(a, axes, size):
    wide = jnp.broadcast_to(a[None], (size,) + a.shape)
    return lax.all_to_all(wide, axes, 0, 0)


def shards(signal, norm_gain, conv_taps, w_query, w_key, w_value, cotangent):
    zh = lax.axis_index("zh")
    xi = lax.axis_index("x")
    core = lax.axis_index("core")
    pos = jnp.stack([zh, xi, core]).astype(jnp.int32)
    first = core == 0
    sig = signal[0]
    cot = cotangent[0]
    gain = norm_gain.reshape(1, C)

    def halves(a):
        low, high = a[:, :HALF], a[:, HALF:]
        return jnp.where(first, low, high), jnp.where(first, high, low)

    keep, give = halves(cot)
    got = swap(give, "core")
    cot_own = jnp.concatenate(
        [jnp.where(first, keep, got), jnp.where(first, got, keep)], axis=1
    )
    sig_z = swap(sig, "zh")
    parts = [halves(w) for w in (w_query, w_key, w_value)]
    w_own = jnp.concatenate([p[0] for p in parts], axis=1)
    w_oth = jnp.concatenate([p[1] for p in parts], axis=1)
    cots = lax.all_gather(cot_own, ("zh", "x"), axis=0)
    sig_z, cot_own, w_own, w_oth = lax.optimization_barrier((sig_z, cot_own, w_own, w_oth))
    near = share(jnp.concatenate([sig, sig_z], axis=0), "x", 4)
    other = swap(near, "core")

    head_shape = jax.ShapeDtypeStruct((OWN_HEADS, BINS, HEAD_DIM), BF16)
    q, k, v, ext = call(
        hidden_body,
        (head_shape, head_shape, head_shape, jax.ShapeDtypeStruct((160, C), BF16)),
        (pos, near, other, w_own, gain, conv_taps),
        (VM((CHUNKS, CHUNK, C), BF16), VM((288, C), F32), VM((CHUNK, C), BF16)),
    )
    part = jax.ShapeDtypeStruct((OWN_HEADS, CHUNK, HEAD_DIM), BF16)
    dq, stats = call(
        forward_body,
        (part, jax.ShapeDtypeStruct((8, CHUNK), F32)),
        (q, k, v, cot_own),
        (
            VM((OWN_HEADS, CHUNK, HEAD_DIM), BF16),
            VM((CHUNK, BINS), F32),
            VM((CHUNK, 128), F32),
        ),
    )
    stats, cots = lax.optimization_barrier((stats, cots))
    stats_all = share(stats, ("zh", "x"), 8)
    grads = jax.ShapeDtypeStruct((WINDOW, 3 * HALF), BF16)
    mine, give = call(
        backward_body,
        (grads, grads),
        (pos, q, k, v, dq, cots, stats_all),
        (
            VM((OWN_HEADS, BINS, HEAD_DIM), BF16),
            VM((WIDE, 3 * HALF), BF16),
            VM((OWN_HEADS, WIDE, HEAD_DIM), BF16),
            VM((OWN_HEADS, WIDE, HEAD_DIM), BF16),
            VM((OWN_HEADS, 2 * EDGE, HEAD_DIM), BF16),
            VM((OWN_HEADS, 2 * EDGE, HEAD_DIM), BF16),
            VM((2 * EDGE, 128), F32),
        ),
    )
    recv = swap(give, "core")
    out, usum = call(
        conv_body,
        (jax.ShapeDtypeStruct((BLOCK, C), BF16), jax.ShapeDtypeStruct((2, 16, 128), F32)),
        (pos, mine, recv, w_own, w_oth, ext, gain, conv_taps),
        (VM((WINDOW, C), F32), VM((WINDOW, C), F32), VM((WINDOW, C), F32)),
    )
    wide = jnp.broadcast_to(usum[None], (16, 2, 16, 128)).reshape(32, 16, 128)
    part = jnp.sum(lax.all_to_all(wide, ("y", "x", "core"), 0, 0), axis=0)
    part = share(part.astype(BF16), ("zm", "zl", "zh"), 16).astype(F32)
    part = jnp.sum(part, axis=0)
    usum = lax.all_gather(part, "core", axis=0)[:, :15].reshape(2, 5, HALF)
    usum = jnp.concatenate([usum[0], usum[1]], axis=1)
    grad_taps = usum * gain
    grad_gain = jnp.sum(usum * conv_taps, axis=0)
    return out[None], grad_taps, grad_gain


def solution(mesh):
    shape = (mesh.devices.size // 128, 2, 4, 2, 4, 2)
    fine = Mesh(mesh.devices.reshape(shape), AXES)
    rows = P(("y", "zm", "zl"), ("zh", "x", "core"), None)
    in_specs = (rows, P(), P(), P(), P(), P(), rows)
    out_specs = (rows, P(), P())
    return jax.shard_map(shards, mesh=fine, in_specs=in_specs, out_specs=out_specs, check_vma=False)
```

```python
import math

import jax
import jax.numpy as jnp
from jax import lax
from jax.experimental import pallas as pl
from jax.experimental.pallas import tpu as pltpu
from jax.sharding import Mesh
from jax.sharding import PartitionSpec as P

HEADS = 6
HEAD_DIM = 128
OWN_HEADS = 3
HALF = OWN_HEADS * HEAD_DIM
EPSILON = 1e-06
GELU_ROOT = math.sqrt(2.0 / math.pi)
SCALE = 1.0 / math.sqrt(HEAD_DIM)
BLOCK = 128
CHUNK = 256
CHUNKS = 8
BINS = 2048
C = 768
INTERPRET = False
F32 = jnp.float32
BF16 = jnp.bfloat16
VM = pltpu.VMEM


def vspec():
    return pl.BlockSpec(memory_space=pltpu.VMEM)


def sspec():
    return pl.BlockSpec(memory_space=pltpu.SMEM)


def call(body, out_shape, args, scratch=(), limit=16):
    specs = [sspec() if a.dtype == jnp.int32 else vspec() for a in args]
    outs = jax.tree.map(lambda _: vspec(), out_shape)
    return pl.pallas_call(
        body,
        out_shape=out_shape,
        in_specs=specs,
        out_specs=outs,
        scratch_shapes=list(scratch),
        compiler_params=pltpu.CompilerParams(vmem_limit_bytes=limit << 20),
        interpret=INTERPRET,
    )(*args)


def nt(a, b):
    return lax.dot_general(a, b, (((1,), (1,)), ((), ())), preferred_element_type=F32)


def nn(a, b):
    return lax.dot_general(a, b, (((1,), (0,)), ((), ())), preferred_element_type=F32)


def neighbours(pos, dz, dx):
    zh = pos[0]
    xa = lax.rem(pos[1] + dx, 4)
    za = lax.rem(zh + dz, 2)
    wrap_lo = (xa == 0).astype(jnp.int32)
    wrap_hi = (xa == 3).astype(jnp.int32)
    prev = lax.rem(dz + wrap_lo, 2) * 4 + lax.rem(dx + 3, 4)
    nxt = lax.rem(dz + wrap_hi, 2) * 4 + lax.rem(dx + 1, 4)
    prev_ok = 1 - wrap_lo * (1 - za)
    nxt_ok = 1 - wrap_hi * za
    return prev, nxt, prev_ok.astype(F32), nxt_ok.astype(F32)


def normalize(rows):
    return rows * lax.rsqrt(jnp.mean(rows * rows, axis=-1, keepdims=True) + EPSILON)


def hidden_body(
    pos, near, other, w, taps, q, k, v, ext, xs, ns, hs
):
    core = pos[2]
    here = pl.multiple_of(core * BLOCK, BLOCK)
    there = pl.multiple_of((1 - core) * BLOCK, BLOCK)
    for c in range(CHUNKS):
        xa = lax.rem(pos[1] + c % 4, 4)
        sl = slice((c // 4) * BLOCK, (c // 4 + 1) * BLOCK)
        xs[c, pl.ds(here, BLOCK), :] = near[xa, sl, :]
        xs[c, pl.ds(there, BLOCK), :] = other[xa, sl, :]
    prev, nxt, prev_ok, nxt_ok = neighbours(pos, jnp.int32(0), jnp.int32(0))
    first = core == 0
    ext[16:144, :] = near[pos[1], 0:BLOCK, :]

    @pl.when(first)
    def _():
        ext[0:16, :] = (xs[prev, 240:256, :].astype(F32) * prev_ok).astype(BF16)
        ext[144:160, :] = xs[0, 128:144, :]

    @pl.when(jnp.logical_not(first))
    def _():
        ext[0:16, :] = xs[0, 112:128, :]
        ext[144:160, :] = (xs[nxt, 0:16, :].astype(F32) * nxt_ok).astype(BF16)

    def chunk(c, _):
        dz = lax.div(c, 4)
        dx = lax.rem(c, 4)
        prev, nxt, prev_ok, nxt_ok = neighbours(pos, dz, dx)
        g = taps[5:6, :]
        ns[0:16, :] = normalize(xs[prev, 240:256, :].astype(F32)) * g * prev_ok
        ns[272:288, :] = normalize(xs[nxt, 0:16, :].astype(F32)) * g * nxt_ok
        for r in range(0, CHUNK, 16):
            ns[16 + r : 32 + r, :] = normalize(xs[c, r : r + 16, :].astype(F32)) * g
        for j in range(0, C, 128):
            tap = [taps[t : t + 1, j : j + 128] for t in range(5)]
            for r in range(0, CHUNK, 64):
                u = tap[0] * ns[14 + r : 78 + r, j : j + 128]
                for t in range(1, 5):
                    u = u + tap[t] * ns[14 + r + t : 78 + r + t, j : j + 128]
                inner = GELU_ROOT * (u + 0.044715 * u * u * u)
                act = 0.5 * u * (1.0 + jnp.tanh(inner))
                x = xs[c, r : r + 64, j : j + 128].astype(F32)
                hs[r : r + 64, j : j + 128] = (x + act).astype(BF16)
        y = nn(hs[...], w[...]).astype(BF16)
        at = pl.multiple_of(c * CHUNK, CHUNK)
        for h in range(OWN_HEADS):
            q[h, pl.ds(at, CHUNK), :] = y[:, h * 128 : (h + 1) * 128]
            k[h, pl.ds(at, CHUNK), :] = y[:, HALF + h * 128 : HALF + (h + 1) * 128]
            v[h, pl.ds(at, CHUNK), :] = y[:, 2 * HALF + h * 128 : 2 * HALF + (h + 1) * 128]
        return 0

    lax.fori_loop(0, CHUNKS, chunk, 0)


KB = 512


def forward_body(q, k, v, d0, d4, dq, stats, ds, ss, sm):
    for g, d in enumerate((d0, d4)):
        for h in range(OWN_HEADS):
            ds[h, g * CHUNK : g * CHUNK + BLOCK, :] = d[0:BLOCK, h * 128 : (h + 1) * 128]
            ds[h, g * CHUNK + BLOCK : (g + 1) * CHUNK, :] = d[
                0:BLOCK, HALF + h * 128 : HALF + (h + 1) * 128
            ]
    sm[...] = jnp.zeros_like(sm)
    lane = lax.broadcasted_iota(jnp.int32, (CHUNK, 128), 1)

    def head(h, _):
        for g in range(2):
            qh = q[h, g * 1024 : g * 1024 + CHUNK, :]
            top = None
            for b in range(0, BINS, KB):
                s = nt(qh, k[h, b : b + KB, :])
                ss[:, b : b + KB] = s
                m = jnp.max(s, axis=1, keepdims=True)
                top = m if top is None else jnp.maximum(top, m)
            total = jnp.zeros((CHUNK, 1), F32)
            out = jnp.zeros((CHUNK, HEAD_DIM), F32)
            for b in range(0, BINS, KB):
                p = jnp.exp((ss[:, b : b + KB] - top) * SCALE)
                total = total + jnp.sum(p, axis=1, keepdims=True)
                out = out + nn(p.astype(BF16), v[h, b : b + KB, :])
                if g == 0:
                    ss[:, b : b + KB] = p
            inverse = 1.0 / total
            attended = (out * inverse).astype(BF16).astype(F32)
            do = ds[h, g * CHUNK : (g + 1) * CHUNK, :]
            delta = jnp.sum(do.astype(F32) * attended, axis=1, keepdims=True)
            log_total = top * SCALE + jnp.log(total)
            sl = slice(g * CHUNK, (g + 1) * CHUNK)
            sm[sl, :] = jnp.where(
                lane == h, log_total, jnp.where(lane == h + OWN_HEADS, delta, sm[sl, :])
            )
            if g == 0:
                acc = jnp.zeros((CHUNK, HEAD_DIM), F32)
                for b in range(0, BINS, KB):
                    dp = nt(do, v[h, b : b + KB, :])
                    dsc = (ss[:, b : b + KB] * inverse * (dp - delta)).astype(BF16)
                    acc = acc + nn(dsc, k[h, b : b + KB, :])
                dq[h, :, :] = (acc * SCALE).astype(BF16)
        return 0

    lax.fori_loop(0, OWN_HEADS, head, 0)
    stats[...] = jnp.transpose(sm[...])[0:8, :]


EDGE = 16
WIDE = CHUNK + 2 * EDGE
WINDOW = BLOCK + 2 * EDGE


def backward_body(
    pos, q, k, v, dq, d0, d4, b1, b2, b3, stats, mine, give, ds, gs, kx, vx, qx, dx_, st
):
    core = pos[2]

    def place(c):
        return lax.rem(pos[1] + c, 4)

    blocks = ((d0, 0), (b1, 0), (b2, 0), (b3, 0), (d4, 0), (b1, BLOCK), (b2, BLOCK), (b3, BLOCK))
    for c, (d, low) in enumerate(blocks):
        for h in range(OWN_HEADS):
            lo = c * CHUNK
            rows = slice(low, low + BLOCK)
            ds[h, lo : lo + BLOCK, :] = d[rows, h * 128 : (h + 1) * 128]
            ds[h, lo + BLOCK : lo + CHUNK, :] = d[rows, HALF + h * 128 : HALF + (h + 1) * 128]
    prev, nxt, _, _ = neighbours(pos, jnp.int32(0), jnp.int32(0))
    low = pl.multiple_of(prev * CHUNK + CHUNK - EDGE, EDGE)
    high = pl.multiple_of(nxt * CHUNK, EDGE)
    for h in range(OWN_HEADS):
        for src, dst in ((k, kx), (v, vx)):
            dst[h, 0:EDGE, :] = src[h, pl.ds(low, EDGE), :]
            dst[h, EDGE : EDGE + CHUNK, :] = src[h, 0:CHUNK, :]
            dst[h, EDGE + CHUNK : WIDE, :] = src[h, pl.ds(high, EDGE), :]
        for src, dst in ((q, qx), (ds, dx_)):
            dst[h, 0:EDGE, :] = src[h, pl.ds(low, EDGE), :]
            dst[h, EDGE : 2 * EDGE, :] = src[h, pl.ds(high, EDGE), :]
    low_half, high_half = lax.div(prev, 4), lax.div(nxt, 4)
    low_rows = jnp.where(low_half == 0, stats[place(prev), :, 128:256], stats[place(prev), :, 384:512])
    high_rows = jnp.where(high_half == 0, stats[place(nxt), :, 0:128], stats[place(nxt), :, 256:384])
    low_stats = jnp.transpose(jnp.tile(low_rows, (16, 1)))
    high_stats = jnp.transpose(jnp.tile(high_rows, (16, 1)))
    st[0:EDGE, :] = low_stats[128 - EDGE : 128, :]
    st[EDGE : 2 * EDGE, :] = high_stats[0:EDGE, :]
    for h in range(OWN_HEADS):
        kh = kx[h]
        vh = vx[h]

        def step(dx, carry):
            acc_k, acc_v = carry
            for dz in range(2):
                c = dz * 4 + dx
                at = pl.multiple_of(c * CHUNK, CHUNK)
                qc = q[h, pl.ds(at, CHUNK), :]
                dc = ds[h, pl.ds(at, CHUNK), :]
                row = place(c)
                lanes = slice(dz * CHUNK, (dz + 1) * CHUNK)
                log_total = stats[row, h : h + 1, lanes]
                delta = stats[row, h + OWN_HEADS : h + OWN_HEADS + 1, lanes]
                p = jnp.exp(nt(kh, qc) * SCALE - log_total)
                acc_v = acc_v + nn(p.astype(BF16), dc)
                dsc = (p * (nt(vh, dc) - delta)).astype(BF16)
                acc_k = acc_k + nn(dsc, qc)
            return acc_k, acc_v

        zero = jnp.zeros((WIDE, HEAD_DIM), F32)
        acc_k, acc_v = lax.fori_loop(0, 4, step, (zero, zero))
        p = jnp.exp(nt(qx[h], k[h]) * SCALE - st[:, h : h + 1])
        dsc = (p * (nt(dx_[h], v[h]) - st[:, h + OWN_HEADS : h + OWN_HEADS + 1])).astype(BF16)
        dqx = (nn(dsc, k[h]) * SCALE).astype(BF16)
        cols = slice(h * 128, (h + 1) * 128)
        gs[0:EDGE, cols] = dqx[0:EDGE]
        gs[EDGE : EDGE + CHUNK, cols] = dq[h]
        gs[EDGE + CHUNK : WIDE, cols] = dqx[EDGE : 2 * EDGE]
        gs[:, HALF + h * 128 : HALF + (h + 1) * 128] = (acc_k * SCALE).astype(BF16)
        gs[:, 2 * HALF + h * 128 : 2 * HALF + (h + 1) * 128] = acc_v.astype(BF16)
    mine[...] = gs[pl.ds(pl.multiple_of(core * BLOCK, BLOCK), WINDOW), :]
    give[...] = gs[pl.ds(pl.multiple_of((1 - core) * BLOCK, BLOCK), WINDOW), :]


def conv_body(pos, mine, recv, w_own, w_oth, ext, taps, out, usum, ns, gh, gc):
    _, _, prev_ok, nxt_ok = neighbours(pos, jnp.int32(0), jnp.int32(0))
    first = pos[2] == 0
    low_ok = jnp.where(first, prev_ok, 1.0)
    high_ok = jnp.where(first, 1.0, nxt_ok)
    g = taps[5:6, :]
    for r in range(0, WINDOW, 16):
        ns[r : r + 16, :] = normalize(ext[r : r + 16, :].astype(F32))
    gh[...] = nt(mine[...], w_own[...]) + nt(recv[...], w_oth[...])
    for j in range(0, C, 128):
        tap = [taps[t : t + 1, j : j + 128] for t in range(5)]
        gj = g[:, j : j + 128]
        cols = slice(j, j + 128)

        def grad(r, n):
            near = [ns[r - 2 + t : r - 2 + t + n, cols] for t in range(5)]
            u = tap[0] * (near[0] * gj)
            for t in range(1, 5):
                u = u + tap[t] * (near[t] * gj)
            inner = GELU_ROOT * (u + 0.044715 * u * u * u)
            th = jnp.tanh(inner)
            slope = 0.5 * (1.0 + th) + 0.5 * u * (1.0 - th * th) * GELU_ROOT * (
                1.0 + 3.0 * 0.044715 * u * u
            )
            return near, gh[r : r + n, cols] * slope

        _, edge = grad(8, 8)
        gc[8:16, cols] = edge * low_ok
        _, edge = grad(144, 8)
        gc[144:152, cols] = edge * high_ok
        sums = [jnp.zeros((8, 128), F32) for _ in range(5)]
        for r in range(EDGE, EDGE + BLOCK, 64):
            near, val = grad(r, 64)
            gc[r : r + 64, cols] = val
            for t in range(5):
                sums[t] = sums[t] + jnp.sum((val * near[t]).reshape(8, 8, 128), axis=0)
        side, slot = divmod(j // 128, OWN_HEADS)
        for t in range(5):
            row = t * OWN_HEADS + slot
            usum[side, row : row + 1, :] = jnp.sum(sums[t], axis=0, keepdims=True)
    usum[:, 15:16, :] = jnp.zeros((2, 1, 128), F32)
    tap = [taps[t : t + 1, :] for t in range(5)]
    for r in range(EDGE, EDGE + BLOCK, 16):
        gn = tap[0] * gc[r + 2 : r + 18, :]
        for t in range(1, 5):
            gn = gn + tap[t] * gc[r + 2 - t : r + 18 - t, :]
        x = ext[r : r + 16, :].astype(F32)
        inv = lax.rsqrt(jnp.mean(x * x, axis=-1, keepdims=True) + EPSILON)
        scaled = gn * g
        inner = jnp.mean(scaled * x, axis=-1, keepdims=True)
        res = gh[r : r + 16, :] + inv * scaled - x * (inv * inv * inv * inner)
        out[r - EDGE : r - EDGE + 16, :] = res.astype(BF16)


AXES = ("y", "zm", "zl", "zh", "x", "core")


def swap(a, axis):
    return lax.ppermute(a, axis, [(0, 1), (1, 0)])


def from_x(a, step):
    return lax.ppermute(a, "x", [((i + step) % 4, i) for i in range(4)])


def share(a, axes, size):
    wide = jnp.broadcast_to(a[None], (size,) + a.shape)
    return lax.all_to_all(wide, axes, 0, 0)


def shards(signal, norm_gain, conv_taps, w_query, w_key, w_value, cotangent):
    zh = lax.axis_index("zh")
    xi = lax.axis_index("x")
    core = lax.axis_index("core")
    pos = jnp.stack([zh, xi, core]).astype(jnp.int32)
    first = core == 0
    sig = signal[0]
    cot = cotangent[0]
    gain = norm_gain.reshape(1, C)

    def halves(a):
        low, high = a[:, :HALF], a[:, HALF:]
        return jnp.where(first, low, high), jnp.where(first, high, low)

    keep, give = halves(cot)
    got = swap(give, "core")
    cot_own = jnp.concatenate(
        [jnp.where(first, keep, got), jnp.where(first, got, keep)], axis=1
    )
    sig_z = swap(sig, "zh")
    parts = [halves(w) for w in (w_query, w_key, w_value)]
    w_own = jnp.concatenate([p[0] for p in parts], axis=1)
    w_oth = jnp.concatenate([p[1] for p in parts], axis=1)
    coef = jnp.concatenate([conv_taps, gain, jnp.zeros((2, C), F32)], axis=0)
    sig_z, cot_own, w_own, w_oth, coef = lax.optimization_barrier(
        (sig_z, cot_own, w_own, w_oth, coef)
    )
    cot_z = swap(cot_own, "zh")
    near = share(jnp.concatenate([sig, sig_z], axis=0), "x", 4)
    near, cot_z = lax.optimization_barrier((near, cot_z))
    other = swap(near, "core")
    both = jnp.concatenate([cot_own, cot_z], axis=0)
    cots = [from_x(both, d) for d in (1, 2, 3)]

    head_shape = jax.ShapeDtypeStruct((OWN_HEADS, BINS, HEAD_DIM), BF16)
    q, k, v, ext = call(
        hidden_body,
        (head_shape, head_shape, head_shape, jax.ShapeDtypeStruct((160, C), BF16)),
        (pos, near, other, w_own, coef),
        (VM((CHUNKS, CHUNK, C), BF16), VM((288, C), F32), VM((CHUNK, C), BF16)),
    )
    part = jax.ShapeDtypeStruct((OWN_HEADS, CHUNK, HEAD_DIM), BF16)
    dq, stats = call(
        forward_body,
        (part, jax.ShapeDtypeStruct((8, 2 * CHUNK), F32)),
        (q, k, v, cot_own, cot_z),
        (
            VM((OWN_HEADS, 2 * CHUNK, HEAD_DIM), BF16),
            VM((CHUNK, BINS), F32),
            VM((2 * CHUNK, 128), F32),
        ),
    )
    stats, cots = lax.optimization_barrier((stats, cots))
    stats_all = share(stats, "x", 4)
    grads = jax.ShapeDtypeStruct((WINDOW, 3 * HALF), BF16)
    mine, give = call(
        backward_body,
        (grads, grads),
        (pos, q, k, v, dq, cot_own, cot_z, *cots, stats_all),
        (
            VM((OWN_HEADS, BINS, HEAD_DIM), BF16),
            VM((WIDE, 3 * HALF), BF16),
            VM((OWN_HEADS, WIDE, HEAD_DIM), BF16),
            VM((OWN_HEADS, WIDE, HEAD_DIM), BF16),
            VM((OWN_HEADS, 2 * EDGE, HEAD_DIM), BF16),
            VM((OWN_HEADS, 2 * EDGE, HEAD_DIM), BF16),
            VM((2 * EDGE, 128), F32),
        ),
    )
    recv = swap(give, "core")
    out, usum = call(
        conv_body,
        (jax.ShapeDtypeStruct((BLOCK, C), BF16), jax.ShapeDtypeStruct((2, 16, 128), F32)),
        (pos, mine, recv, w_own, w_oth, ext, coef),
        (VM((WINDOW, C), F32), VM((WINDOW, C), F32), VM((WINDOW, C), F32)),
    )
    wide = jnp.broadcast_to(usum[None], (16, 2, 16, 128)).reshape(32, 16, 128)
    part = jnp.sum(lax.all_to_all(wide, ("y", "x", "core"), 0, 0), axis=0)
    part = share(part.astype(BF16), ("zm", "zl", "zh"), 16).astype(F32)
    part = jnp.sum(part, axis=0)
    usum = lax.all_gather(part, "core", axis=0)[:, :15].reshape(2, 5, HALF)
    usum = jnp.concatenate([usum[0], usum[1]], axis=1)
    grad_taps = usum * gain
    grad_gain = jnp.sum(usum * conv_taps, axis=0)
    return out[None], grad_taps, grad_gain


def solution(mesh):
    shape = (mesh.devices.size // 128, 2, 4, 2, 4, 2)
    fine = Mesh(mesh.devices.reshape(shape), AXES)
    rows = P(("y", "zm", "zl"), ("zh", "x", "core"), None)
    in_specs = (rows, P(), P(), P(), P(), P(), rows)
    out_specs = (rows, P(), P())
    return jax.shard_map(shards, mesh=fine, in_specs=in_specs, out_specs=out_specs, check_vma=False)
```

```python
import math

import jax
import jax.numpy as jnp
from jax import lax
from jax.experimental import pallas as pl
from jax.experimental.pallas import tpu as pltpu
from jax.sharding import Mesh
from jax.sharding import PartitionSpec as P

HEADS = 6
HEAD_DIM = 128
OWN_HEADS = 3
HALF = OWN_HEADS * HEAD_DIM
EPSILON = 1e-06
GELU_ROOT = math.sqrt(2.0 / math.pi)
SCALE = 1.0 / math.sqrt(HEAD_DIM)
BLOCK = 128
CHUNK = 256
CHUNKS = 8
BINS = 2048
C = 768
INTERPRET = False
F32 = jnp.float32
BF16 = jnp.bfloat16
VM = pltpu.VMEM


def vspec():
    return pl.BlockSpec(memory_space=pltpu.VMEM)


def sspec():
    return pl.BlockSpec(memory_space=pltpu.SMEM)


def call(body, out_shape, args, scratch=(), limit=16, held=()):
    specs = [sspec() if a.dtype == jnp.int32 else vspec() for a in args]
    for i in held:
        specs[i] = pl.BlockSpec(memory_space=pltpu.HBM)
    outs = jax.tree.map(lambda _: vspec(), out_shape)
    return pl.pallas_call(
        body,
        out_shape=out_shape,
        in_specs=specs,
        out_specs=outs,
        scratch_shapes=list(scratch),
        compiler_params=pltpu.CompilerParams(vmem_limit_bytes=limit << 20),
        interpret=INTERPRET,
    )(*args)


def nt(a, b):
    return lax.dot_general(a, b, (((1,), (1,)), ((), ())), preferred_element_type=F32)


def nn(a, b):
    return lax.dot_general(a, b, (((1,), (0,)), ((), ())), preferred_element_type=F32)


def neighbours(pos, dz, dx):
    zh = pos[0]
    xa = lax.rem(pos[1] + dx, 4)
    za = lax.rem(zh + dz, 2)
    wrap_lo = (xa == 0).astype(jnp.int32)
    wrap_hi = (xa == 3).astype(jnp.int32)
    prev = lax.rem(dz + wrap_lo, 2) * 4 + lax.rem(dx + 3, 4)
    nxt = lax.rem(dz + wrap_hi, 2) * 4 + lax.rem(dx + 1, 4)
    prev_ok = 1 - wrap_lo * (1 - za)
    nxt_ok = 1 - wrap_hi * za
    return prev, nxt, prev_ok.astype(F32), nxt_ok.astype(F32)


def normalize(rows):
    return rows * lax.rsqrt(jnp.mean(rows * rows, axis=-1, keepdims=True) + EPSILON)


def activate(ns, r, n, cols, tap):
    u = tap[0] * ns[r - 2 : r - 2 + n, cols]
    for t in range(1, 5):
        u = u + tap[t] * ns[r - 2 + t : r - 2 + t + n, cols]
    inner = GELU_ROOT * (u + 0.044715 * u * u * u)
    return 0.5 * u * (1.0 + jnp.tanh(inner))


def hidden_chunk(xs, c, low, high, taps, ns, hs):
    g = taps[5:6, :]
    ns[0:16, :] = normalize(low) * g
    ns[272:288, :] = normalize(high) * g
    for r in range(0, CHUNK, 16):
        ns[16 + r : 32 + r, :] = normalize(xs[c, r : r + 16, :].astype(F32)) * g
    for j in range(0, C, 128):
        tap = [taps[t : t + 1, j : j + 128] for t in range(5)]
        cols = slice(j, j + 128)
        for r in range(0, CHUNK, 64):
            act = activate(ns, 16 + r, 64, cols, tap)
            x = xs[c, r : r + 64, cols].astype(F32)
            hs[r : r + 64, cols] = (x + act).astype(BF16)


def project(rows, w, q, k, v, at, n):
    y = nn(rows, w[...]).astype(BF16)
    for h in range(OWN_HEADS):
        q[h, pl.ds(at, n), :] = y[:, h * 128 : (h + 1) * 128]
        k[h, pl.ds(at, n), :] = y[:, HALF + h * 128 : HALF + (h + 1) * 128]
        v[h, pl.ds(at, n), :] = y[:, 2 * HALF + h * 128 : 2 * HALF + (h + 1) * 128]


def assemble(pos, near, other, xs):
    here = pl.multiple_of(pos[2] * BLOCK, BLOCK)
    there = pl.multiple_of((1 - pos[2]) * BLOCK, BLOCK)
    for c in range(4):
        xa = lax.rem(pos[1] + c, 4)
        xs[c, pl.ds(here, BLOCK), :] = near[xa]
        xs[c, pl.ds(there, BLOCK), :] = other[xa]


def own_half_body(pos, near, other, w, taps, q, k, v, xs, ns, hs):
    assemble(pos, near, other, xs)

    def chunk(c, _):
        xa = lax.rem(pos[1] + c, 4)
        low = xs[lax.rem(c + 3, 4), 240:256, :].astype(F32) * (xa > 0).astype(F32)
        high = xs[lax.rem(c + 1, 4), 0:16, :].astype(F32) * (xa < 3).astype(F32)
        hidden_chunk(xs, c, low, high, taps, ns, hs)
        project(hs[...], w, q, k, v, pl.multiple_of(c * CHUNK, CHUNK), CHUNK)
        return 0

    lax.fori_loop(0, 4, chunk, 0)


def far_half_body(
    pos, near, other, own_in, q0, k0, v0, w, taps, q, k, v, ext, xs, ns, hs, rs, own, sem
):
    pairs = ((own_in, own), (q0, q), (k0, k), (v0, v))
    copies = [
        pltpu.make_async_copy(src, dst if i == 0 else dst.at[:, 0:1024, :], sem.at[i])
        for i, (src, dst) in enumerate(pairs)
    ]
    for copy in copies:
        copy.start()
    assemble(pos, near, other, xs)
    copies[0].wait()
    zh, x, core = pos[0], pos[1], pos[2]

    def chunk(c, _):
        xa = lax.rem(x + c, 4)
        lo, hi = lax.rem(c + 3, 4), lax.rem(c + 1, 4)
        wrap_lo, wrap_hi = (xa == 0).astype(F32), (xa == 3).astype(F32)
        low_ok, high_ok = (zh == 0).astype(F32), (zh == 1).astype(F32)
        low = xs[lo, 240:256, :].astype(F32) * (1.0 - wrap_lo)
        low = low + own[lo, 240:256, :].astype(F32) * (wrap_lo * low_ok)
        high = xs[hi, 0:16, :].astype(F32) * (1.0 - wrap_hi)
        high = high + own[hi, 0:16, :].astype(F32) * (wrap_hi * high_ok)
        hidden_chunk(xs, c, low, high, taps, ns, hs)
        project(hs[...], w, q, k, v, pl.multiple_of(1024 + c * CHUNK, CHUNK), CHUNK)
        return 0

    lax.fori_loop(0, 4, chunk, 0)

    edge = lax.rem(jnp.where(zh == 0, 3, 4) - x, 4)

    @pl.when(zh == 0)
    def _():
        rs[0:32, :] = own[edge, 224:256, :]
        rs[32:48, :] = xs[lax.rem(edge + 1, 4), 0:16, :]

    @pl.when(zh == 1)
    def _():
        rs[0:16, :] = xs[lax.rem(edge + 3, 4), 240:256, :]
        rs[16:48, :] = own[edge, 0:32, :]

    for r in range(0, 48, 16):
        ns[r : r + 16, :] = normalize(rs[r : r + 16, :].astype(F32)) * taps[5:6, :]
    for j in range(0, C, 128):
        tap = [taps[t : t + 1, j : j + 128] for t in range(5)]
        cols = slice(j, j + 128)
        act = activate(ns, 16, 16, cols, tap)
        hs[0:16, cols] = (rs[16:32, cols].astype(F32) + act).astype(BF16)
    for copy in copies[1:]:
        copy.wait()
    at = pl.multiple_of(edge * CHUNK + jnp.where(zh == 0, 240, 0), 16)
    project(hs[0:16, :], w, q, k, v, at, 16)

    ext[16:144, :] = own[0, pl.ds(pl.multiple_of(core * BLOCK, BLOCK), BLOCK), :]

    @pl.when(core == 0)
    def _():
        ext[144:160, :] = own[0, 128:144, :]
        inside = (x > 0).astype(F32)
        across = (1.0 - inside) * (zh == 1).astype(F32)
        low = own[3, 240:256, :].astype(F32) * inside + xs[3, 240:256, :].astype(F32) * across
        ext[0:16, :] = low.astype(BF16)

    @pl.when(core == 1)
    def _():
        ext[0:16, :] = own[0, 112:128, :]
        inside = (x < 3).astype(F32)
        across = (1.0 - inside) * (zh == 0).astype(F32)
        high = own[1, 0:16, :].astype(F32) * inside + xs[1, 0:16, :].astype(F32) * across
        ext[144:160, :] = high.astype(BF16)


KB = 512


def forward_body(q, k, v, d0, d4, dq, stats, ds, ss, sm):
    for g, d in enumerate((d0, d4)):
        for h in range(OWN_HEADS):
            ds[h, g * CHUNK : g * CHUNK + BLOCK, :] = d[0:BLOCK, h * 128 : (h + 1) * 128]
            ds[h, g * CHUNK + BLOCK : (g + 1) * CHUNK, :] = d[
                0:BLOCK, HALF + h * 128 : HALF + (h + 1) * 128
            ]
    sm[...] = jnp.zeros_like(sm)
    lane = lax.broadcasted_iota(jnp.int32, (CHUNK, 128), 1)

    def head(h, _):
        for g in range(2):
            qh = q[h, g * 1024 : g * 1024 + CHUNK, :]
            top = None
            for b in range(0, BINS, KB):
                s = nt(qh, k[h, b : b + KB, :])
                ss[:, b : b + KB] = s
                m = jnp.max(s, axis=1, keepdims=True)
                top = m if top is None else jnp.maximum(top, m)
            total = jnp.zeros((CHUNK, 1), F32)
            out = jnp.zeros((CHUNK, HEAD_DIM), F32)
            for b in range(0, BINS, KB):
                p = jnp.exp((ss[:, b : b + KB] - top) * SCALE)
                total = total + jnp.sum(p, axis=1, keepdims=True)
                out = out + nn(p.astype(BF16), v[h, b : b + KB, :])
                if g == 0:
                    ss[:, b : b + KB] = p
            inverse = 1.0 / total
            attended = (out * inverse).astype(BF16).astype(F32)
            do = ds[h, g * CHUNK : (g + 1) * CHUNK, :]
            delta = jnp.sum(do.astype(F32) * attended, axis=1, keepdims=True)
            log_total = top * SCALE + jnp.log(total)
            sl = slice(g * CHUNK, (g + 1) * CHUNK)
            sm[sl, :] = jnp.where(
                lane == h, log_total, jnp.where(lane == h + OWN_HEADS, delta, sm[sl, :])
            )
            if g == 0:
                acc = jnp.zeros((CHUNK, HEAD_DIM), F32)
                for b in range(0, BINS, KB):
                    dp = nt(do, v[h, b : b + KB, :])
                    dsc = (ss[:, b : b + KB] * inverse * (dp - delta)).astype(BF16)
                    acc = acc + nn(dsc, k[h, b : b + KB, :])
                dq[h, :, :] = (acc * SCALE).astype(BF16)
        return 0

    lax.fori_loop(0, OWN_HEADS, head, 0)
    stats[...] = jnp.transpose(sm[...])[0:8, :]


EDGE = 16
WIDE = CHUNK + 2 * EDGE
WINDOW = BLOCK + 2 * EDGE


def backward_body(
    pos, q, k, v, dq, d0, d4, b1, b2, b3, stats, mine, give, ds, gs, kx, vx, qx, dx_, st
):
    core = pos[2]

    def place(c):
        return lax.rem(pos[1] + c, 4)

    blocks = ((d0, 0), (b1, 0), (b2, 0), (b3, 0), (d4, 0), (b1, BLOCK), (b2, BLOCK), (b3, BLOCK))
    for c, (d, low) in enumerate(blocks):
        for h in range(OWN_HEADS):
            lo = c * CHUNK
            rows = slice(low, low + BLOCK)
            ds[h, lo : lo + BLOCK, :] = d[rows, h * 128 : (h + 1) * 128]
            ds[h, lo + BLOCK : lo + CHUNK, :] = d[rows, HALF + h * 128 : HALF + (h + 1) * 128]
    prev, nxt, _, _ = neighbours(pos, jnp.int32(0), jnp.int32(0))
    low = pl.multiple_of(prev * CHUNK + CHUNK - EDGE, EDGE)
    high = pl.multiple_of(nxt * CHUNK, EDGE)
    for h in range(OWN_HEADS):
        for src, dst in ((k, kx), (v, vx)):
            dst[h, 0:EDGE, :] = src[h, pl.ds(low, EDGE), :]
            dst[h, EDGE : EDGE + CHUNK, :] = src[h, 0:CHUNK, :]
            dst[h, EDGE + CHUNK : WIDE, :] = src[h, pl.ds(high, EDGE), :]
        for src, dst in ((q, qx), (ds, dx_)):
            dst[h, 0:EDGE, :] = src[h, pl.ds(low, EDGE), :]
            dst[h, EDGE : 2 * EDGE, :] = src[h, pl.ds(high, EDGE), :]
    low_half, high_half = lax.div(prev, 4), lax.div(nxt, 4)
    low_rows = jnp.where(low_half == 0, stats[place(prev), :, 128:256], stats[place(prev), :, 384:512])
    high_rows = jnp.where(high_half == 0, stats[place(nxt), :, 0:128], stats[place(nxt), :, 256:384])
    low_stats = jnp.transpose(jnp.tile(low_rows, (16, 1)))
    high_stats = jnp.transpose(jnp.tile(high_rows, (16, 1)))
    st[0:EDGE, :] = low_stats[128 - EDGE : 128, :]
    st[EDGE : 2 * EDGE, :] = high_stats[0:EDGE, :]
    for h in range(OWN_HEADS):
        kh = kx[h]
        vh = vx[h]

        def step(dx, carry):
            acc_k, acc_v = carry
            for dz in range(2):
                c = dz * 4 + dx
                at = pl.multiple_of(c * CHUNK, CHUNK)
                qc = q[h, pl.ds(at, CHUNK), :]
                dc = ds[h, pl.ds(at, CHUNK), :]
                row = place(c)
                lanes = slice(dz * CHUNK, (dz + 1) * CHUNK)
                log_total = stats[row, h : h + 1, lanes]
                delta = stats[row, h + OWN_HEADS : h + OWN_HEADS + 1, lanes]
                p = jnp.exp(nt(kh, qc) * SCALE - log_total)
                acc_v = acc_v + nn(p.astype(BF16), dc)
                dsc = (p * (nt(vh, dc) - delta)).astype(BF16)
                acc_k = acc_k + nn(dsc, qc)
            return acc_k, acc_v

        zero = jnp.zeros((WIDE, HEAD_DIM), F32)
        acc_k, acc_v = lax.fori_loop(0, 4, step, (zero, zero))
        p = jnp.exp(nt(qx[h], k[h]) * SCALE - st[:, h : h + 1])
        dsc = (p * (nt(dx_[h], v[h]) - st[:, h + OWN_HEADS : h + OWN_HEADS + 1])).astype(BF16)
        dqx = (nn(dsc, k[h]) * SCALE).astype(BF16)
        cols = slice(h * 128, (h + 1) * 128)
        gs[0:EDGE, cols] = dqx[0:EDGE]
        gs[EDGE : EDGE + CHUNK, cols] = dq[h]
        gs[EDGE + CHUNK : WIDE, cols] = dqx[EDGE : 2 * EDGE]
        gs[:, HALF + h * 128 : HALF + (h + 1) * 128] = (acc_k * SCALE).astype(BF16)
        gs[:, 2 * HALF + h * 128 : 2 * HALF + (h + 1) * 128] = acc_v.astype(BF16)
    mine[...] = gs[pl.ds(pl.multiple_of(core * BLOCK, BLOCK), WINDOW), :]
    give[...] = gs[pl.ds(pl.multiple_of((1 - core) * BLOCK, BLOCK), WINDOW), :]


def conv_body(pos, mine, recv, w_own, w_oth, ext, taps, out, usum, ns, gh, gc):
    _, _, prev_ok, nxt_ok = neighbours(pos, jnp.int32(0), jnp.int32(0))
    first = pos[2] == 0
    low_ok = jnp.where(first, prev_ok, 1.0)
    high_ok = jnp.where(first, 1.0, nxt_ok)
    g = taps[5:6, :]
    for r in range(0, WINDOW, 16):
        ns[r : r + 16, :] = normalize(ext[r : r + 16, :].astype(F32))
    gh[...] = nt(mine[...], w_own[...]) + nt(recv[...], w_oth[...])
    for j in range(0, C, 128):
        tap = [taps[t : t + 1, j : j + 128] for t in range(5)]
        gj = g[:, j : j + 128]
        cols = slice(j, j + 128)

        def grad(r, n):
            near = [ns[r - 2 + t : r - 2 + t + n, cols] for t in range(5)]
            u = tap[0] * (near[0] * gj)
            for t in range(1, 5):
                u = u + tap[t] * (near[t] * gj)
            inner = GELU_ROOT * (u + 0.044715 * u * u * u)
            th = jnp.tanh(inner)
            slope = 0.5 * (1.0 + th) + 0.5 * u * (1.0 - th * th) * GELU_ROOT * (
                1.0 + 3.0 * 0.044715 * u * u
            )
            return near, gh[r : r + n, cols] * slope

        _, edge = grad(8, 8)
        gc[8:16, cols] = edge * low_ok
        _, edge = grad(144, 8)
        gc[144:152, cols] = edge * high_ok
        sums = [jnp.zeros((8, 128), F32) for _ in range(5)]
        for r in range(EDGE, EDGE + BLOCK, 64):
            near, val = grad(r, 64)
            gc[r : r + 64, cols] = val
            for t in range(5):
                sums[t] = sums[t] + jnp.sum((val * near[t]).reshape(8, 8, 128), axis=0)
        side, slot = divmod(j // 128, OWN_HEADS)
        for t in range(5):
            row = t * OWN_HEADS + slot
            usum[side, row : row + 1, :] = jnp.sum(sums[t], axis=0, keepdims=True)
    usum[:, 15:16, :] = jnp.zeros((2, 1, 128), F32)
    tap = [taps[t : t + 1, :] for t in range(5)]
    for r in range(EDGE, EDGE + BLOCK, 16):
        gn = tap[0] * gc[r + 2 : r + 18, :]
        for t in range(1, 5):
            gn = gn + tap[t] * gc[r + 2 - t : r + 18 - t, :]
        x = ext[r : r + 16, :].astype(F32)
        inv = lax.rsqrt(jnp.mean(x * x, axis=-1, keepdims=True) + EPSILON)
        scaled = gn * g
        inner = jnp.mean(scaled * x, axis=-1, keepdims=True)
        res = gh[r : r + 16, :] + inv * scaled - x * (inv * inv * inv * inner)
        out[r - EDGE : r - EDGE + 16, :] = res.astype(BF16)


AXES = ("y", "zm", "zl", "zh", "x", "core")


def swap(a, axis):
    return lax.ppermute(a, axis, [(0, 1), (1, 0)])


def from_x(a, step):
    return lax.ppermute(a, "x", [((i + step) % 4, i) for i in range(4)])


def share(a, axes, size):
    wide = jnp.broadcast_to(a[None], (size,) + a.shape)
    return lax.all_to_all(wide, axes, 0, 0)


def shards(signal, norm_gain, conv_taps, w_query, w_key, w_value, cotangent):
    zh = lax.axis_index("zh")
    xi = lax.axis_index("x")
    core = lax.axis_index("core")
    pos = jnp.stack([zh, xi, core]).astype(jnp.int32)
    first = core == 0
    sig = signal[0]
    cot = cotangent[0]
    gain = norm_gain.reshape(1, C)

    def halves(a):
        low, high = a[:, :HALF], a[:, HALF:]
        return jnp.where(first, low, high), jnp.where(first, high, low)

    keep, give = halves(cot)
    got = swap(give, "core")
    cot_own = jnp.concatenate(
        [jnp.where(first, keep, got), jnp.where(first, got, keep)], axis=1
    )
    sig_z = swap(sig, "zh")
    parts = [halves(w) for w in (w_query, w_key, w_value)]
    w_own = jnp.concatenate([p[0] for p in parts], axis=1)
    w_oth = jnp.concatenate([p[1] for p in parts], axis=1)
    coef = jnp.concatenate([conv_taps, gain, jnp.zeros((2, C), F32)], axis=0)
    near = share(sig, "x", 4)
    sig_z, cot_own, w_own, w_oth, coef, near = lax.optimization_barrier(
        (sig_z, cot_own, w_own, w_oth, coef, near)
    )
    near_other = swap(near, "core")
    cot_z = swap(cot_own, "zh")
    far = share(sig_z, "x", 4)
    half_shape = jax.ShapeDtypeStruct((OWN_HEADS, 1024, HEAD_DIM), BF16)
    rows_shape = jax.ShapeDtypeStruct((4, CHUNK, C), BF16)
    q0, k0, v0, own = call(
        own_half_body,
        (half_shape, half_shape, half_shape, rows_shape),
        (pos, near, near_other, w_own, coef),
        (VM((288, C), F32), VM((CHUNK, C), BF16)),
    )
    far, q0, cot_z = lax.optimization_barrier((far, q0, cot_z))
    far_other = swap(far, "core")
    both = jnp.concatenate([cot_own, cot_z], axis=0)
    cots = [from_x(both, d) for d in (1, 2, 3)]
    head_shape = jax.ShapeDtypeStruct((OWN_HEADS, BINS, HEAD_DIM), BF16)
    q, k, v, ext = call(
        far_half_body,
        (head_shape, head_shape, head_shape, jax.ShapeDtypeStruct((160, C), BF16)),
        (pos, far, far_other, own, q0, k0, v0, w_own, coef),
        (
            VM((4, CHUNK, C), BF16),
            VM((288, C), F32),
            VM((CHUNK, C), BF16),
            VM((48, C), BF16),
            VM((4, CHUNK, C), BF16),
            pltpu.SemaphoreType.DMA((4,)),
        ),
        held=(3, 4, 5, 6),
    )
    part = jax.ShapeDtypeStruct((OWN_HEADS, CHUNK, HEAD_DIM), BF16)
    dq, stats = call(
        forward_body,
        (part, jax.ShapeDtypeStruct((8, 2 * CHUNK), F32)),
        (q, k, v, cot_own, cot_z),
        (
            VM((OWN_HEADS, 2 * CHUNK, HEAD_DIM), BF16),
            VM((CHUNK, BINS), F32),
            VM((2 * CHUNK, 128), F32),
        ),
    )
    stats, cots = lax.optimization_barrier((stats, cots))
    stats_all = share(stats, "x", 4)
    grads = jax.ShapeDtypeStruct((WINDOW, 3 * HALF), BF16)
    mine, give = call(
        backward_body,
        (grads, grads),
        (pos, q, k, v, dq, cot_own, cot_z, *cots, stats_all),
        (
            VM((OWN_HEADS, BINS, HEAD_DIM), BF16),
            VM((WIDE, 3 * HALF), BF16),
            VM((OWN_HEADS, WIDE, HEAD_DIM), BF16),
            VM((OWN_HEADS, WIDE, HEAD_DIM), BF16),
            VM((OWN_HEADS, 2 * EDGE, HEAD_DIM), BF16),
            VM((OWN_HEADS, 2 * EDGE, HEAD_DIM), BF16),
            VM((2 * EDGE, 128), F32),
        ),
    )
    recv = swap(give, "core")
    out, usum = call(
        conv_body,
        (jax.ShapeDtypeStruct((BLOCK, C), BF16), jax.ShapeDtypeStruct((2, 16, 128), F32)),
        (pos, mine, recv, w_own, w_oth, ext, coef),
        (VM((WINDOW, C), F32), VM((WINDOW, C), F32), VM((WINDOW, C), F32)),
    )
    wide = jnp.broadcast_to(usum[None], (16, 2, 16, 128)).reshape(32, 16, 128)
    part = jnp.sum(lax.all_to_all(wide, ("y", "x", "core"), 0, 0), axis=0)
    part = share(part.astype(BF16), ("zm", "zl", "zh"), 16).astype(F32)
    part = jnp.sum(part, axis=0)
    usum = lax.all_gather(part, "core", axis=0)[:, :15].reshape(2, 5, HALF)
    usum = jnp.concatenate([usum[0], usum[1]], axis=1)
    grad_taps = usum * gain
    grad_gain = jnp.sum(usum * conv_taps, axis=0)
    return out[None], grad_taps, grad_gain


def solution(mesh):
    shape = (mesh.devices.size // 128, 2, 4, 2, 4, 2)
    fine = Mesh(mesh.devices.reshape(shape), AXES)
    rows = P(("y", "zm", "zl"), ("zh", "x", "core"), None)
    in_specs = (rows, P(), P(), P(), P(), P(), rows)
    out_specs = (rows, P(), P())
    return jax.shard_map(shards, mesh=fine, in_specs=in_specs, out_specs=out_specs, check_vma=False)
```

```python
import math

import jax
import jax.numpy as jnp
from jax import lax
from jax.experimental import pallas as pl
from jax.experimental.pallas import tpu as pltpu
from jax.sharding import Mesh
from jax.sharding import PartitionSpec as P

HEADS = 6
HEAD_DIM = 128
OWN_HEADS = 3
HALF = OWN_HEADS * HEAD_DIM
EPSILON = 1e-06
GELU_ROOT = math.sqrt(2.0 / math.pi)
SCALE = 1.0 / math.sqrt(HEAD_DIM)
BLOCK = 128
CHUNK = 256
CHUNKS = 8
BINS = 2048
C = 768
INTERPRET = False
F32 = jnp.float32
BF16 = jnp.bfloat16
VM = pltpu.VMEM


def vspec():
    return pl.BlockSpec(memory_space=pltpu.VMEM)


def sspec():
    return pl.BlockSpec(memory_space=pltpu.SMEM)


def call(body, out_shape, args, scratch=(), limit=16):
    specs = [sspec() if a.dtype == jnp.int32 else vspec() for a in args]
    outs = jax.tree.map(lambda _: vspec(), out_shape)
    return pl.pallas_call(
        body,
        out_shape=out_shape,
        in_specs=specs,
        out_specs=outs,
        scratch_shapes=list(scratch),
        compiler_params=pltpu.CompilerParams(vmem_limit_bytes=limit << 20),
        interpret=INTERPRET,
    )(*args)


def nt(a, b):
    return lax.dot_general(a, b, (((1,), (1,)), ((), ())), preferred_element_type=F32)


def nn(a, b):
    return lax.dot_general(a, b, (((1,), (0,)), ((), ())), preferred_element_type=F32)


def neighbours(pos, dz, dx):
    zh = pos[0]
    xa = lax.rem(pos[1] + dx, 4)
    za = lax.rem(zh + dz, 2)
    wrap_lo = (xa == 0).astype(jnp.int32)
    wrap_hi = (xa == 3).astype(jnp.int32)
    prev = lax.rem(dz + wrap_lo, 2) * 4 + lax.rem(dx + 3, 4)
    nxt = lax.rem(dz + wrap_hi, 2) * 4 + lax.rem(dx + 1, 4)
    prev_ok = 1 - wrap_lo * (1 - za)
    nxt_ok = 1 - wrap_hi * za
    return prev, nxt, prev_ok.astype(F32), nxt_ok.astype(F32)


def normalize(rows):
    return rows * lax.rsqrt(jnp.mean(rows * rows, axis=-1, keepdims=True) + EPSILON)


def hidden_body(
    pos, near, far, e0, e1, w, taps, q, k, v, ext, xs, ns, hs
):
    core = pos[2]
    here = pl.multiple_of(core * BLOCK, BLOCK)
    there = pl.multiple_of((1 - core) * BLOCK, BLOCK)
    for c in range(CHUNKS):
        xa = lax.rem(pos[1] + c % 4, 4)
        own, other = ((near, e0), (far, e1))[c // 4]
        xs[c, pl.ds(here, BLOCK), :] = own[xa, 0:BLOCK, :]
        xs[c, pl.ds(there, BLOCK), :] = other[xa, :, 0:C]
    prev, nxt, prev_ok, nxt_ok = neighbours(pos, jnp.int32(0), jnp.int32(0))
    first = core == 0
    ext[16:144, :] = near[pos[1], 0:BLOCK, :]

    @pl.when(first)
    def _():
        ext[0:16, :] = (xs[prev, 240:256, :].astype(F32) * prev_ok).astype(BF16)
        ext[144:160, :] = xs[0, 128:144, :]

    @pl.when(jnp.logical_not(first))
    def _():
        ext[0:16, :] = xs[0, 112:128, :]
        ext[144:160, :] = (xs[nxt, 0:16, :].astype(F32) * nxt_ok).astype(BF16)

    def chunk(c, _):
        dz = lax.div(c, 4)
        dx = lax.rem(c, 4)
        prev, nxt, prev_ok, nxt_ok = neighbours(pos, dz, dx)
        g = taps[5:6, :]
        ns[0:16, :] = normalize(xs[prev, 240:256, :].astype(F32)) * g * prev_ok
        ns[272:288, :] = normalize(xs[nxt, 0:16, :].astype(F32)) * g * nxt_ok
        for r in range(0, CHUNK, 16):
            ns[16 + r : 32 + r, :] = normalize(xs[c, r : r + 16, :].astype(F32)) * g
        for j in range(0, C, 128):
            tap = [taps[t : t + 1, j : j + 128] for t in range(5)]
            for r in range(0, CHUNK, 64):
                u = tap[0] * ns[14 + r : 78 + r, j : j + 128]
                for t in range(1, 5):
                    u = u + tap[t] * ns[14 + r + t : 78 + r + t, j : j + 128]
                inner = GELU_ROOT * (u + 0.044715 * u * u * u)
                act = 0.5 * u * (1.0 + jnp.tanh(inner))
                x = xs[c, r : r + 64, j : j + 128].astype(F32)
                hs[r : r + 64, j : j + 128] = (x + act).astype(BF16)
        y = nn(hs[...], w[...]).astype(BF16)
        at = pl.multiple_of(c * CHUNK, CHUNK)
        for h in range(OWN_HEADS):
            q[h, pl.ds(at, CHUNK), :] = y[:, h * 128 : (h + 1) * 128]
            k[h, pl.ds(at, CHUNK), :] = y[:, HALF + h * 128 : HALF + (h + 1) * 128]
            v[h, pl.ds(at, CHUNK), :] = y[:, 2 * HALF + h * 128 : 2 * HALF + (h + 1) * 128]
        return 0

    lax.fori_loop(0, CHUNKS, chunk, 0)


KB = 512


def cotangents(core, own, other, at, h, dst, row):
    here = pl.multiple_of(row + core * BLOCK, BLOCK)
    there = pl.multiple_of(row + (1 - core) * BLOCK, BLOCK)
    low = own[at, BLOCK:CHUNK, h * 128 : (h + 1) * 128]
    high = own[at, BLOCK:CHUNK, HALF + h * 128 : HALF + (h + 1) * 128]
    dst[h, pl.ds(here, BLOCK), :] = jnp.where(core == 0, low, high)
    dst[h, pl.ds(there, BLOCK), :] = other[at, :, C + h * 128 : C + (h + 1) * 128]


def forward_body(pos, q, k, v, near, far, e0, e1, dq, stats, ds, ss, sm):
    for g, (own, other) in enumerate(((near, e0), (far, e1))):
        for h in range(OWN_HEADS):
            cotangents(pos[2], own, other, pos[1], h, ds, g * CHUNK)
    sm[...] = jnp.zeros_like(sm)
    lane = lax.broadcasted_iota(jnp.int32, (CHUNK, 128), 1)

    def head(h, _):
        for g in range(2):
            qh = q[h, g * 1024 : g * 1024 + CHUNK, :]
            top = None
            for b in range(0, BINS, KB):
                s = nt(qh, k[h, b : b + KB, :])
                ss[:, b : b + KB] = s
                m = jnp.max(s, axis=1, keepdims=True)
                top = m if top is None else jnp.maximum(top, m)
            total = jnp.zeros((CHUNK, 1), F32)
            out = jnp.zeros((CHUNK, HEAD_DIM), F32)
            for b in range(0, BINS, KB):
                p = jnp.exp((ss[:, b : b + KB] - top) * SCALE)
                total = total + jnp.sum(p, axis=1, keepdims=True)
                out = out + nn(p.astype(BF16), v[h, b : b + KB, :])
                if g == 0:
                    ss[:, b : b + KB] = p
            inverse = 1.0 / total
            attended = (out * inverse).astype(BF16).astype(F32)
            do = ds[h, g * CHUNK : (g + 1) * CHUNK, :]
            delta = jnp.sum(do.astype(F32) * attended, axis=1, keepdims=True)
            log_total = top * SCALE + jnp.log(total)
            sl = slice(g * CHUNK, (g + 1) * CHUNK)
            sm[sl, :] = jnp.where(
                lane == h, log_total, jnp.where(lane == h + OWN_HEADS, delta, sm[sl, :])
            )
            if g == 0:
                acc = jnp.zeros((CHUNK, HEAD_DIM), F32)
                for b in range(0, BINS, KB):
                    dp = nt(do, v[h, b : b + KB, :])
                    dsc = (ss[:, b : b + KB] * inverse * (dp - delta)).astype(BF16)
                    acc = acc + nn(dsc, k[h, b : b + KB, :])
                dq[h, :, :] = (acc * SCALE).astype(BF16)
        return 0

    lax.fori_loop(0, OWN_HEADS, head, 0)
    stats[...] = jnp.transpose(sm[...])[0:8, :]


EDGE = 16
WIDE = CHUNK + 2 * EDGE
WINDOW = BLOCK + 2 * EDGE


def backward_body(
    pos, q, k, v, dq, near, far, e0, e1, stats, mine, give, ds, gs, kx, vx, qx, dx_, st
):
    core = pos[2]

    def place(c):
        return lax.rem(pos[1] + c, 4)

    for c in range(CHUNKS):
        own, other = ((near, e0), (far, e1))[c // 4]
        for h in range(OWN_HEADS):
            cotangents(core, own, other, place(jnp.int32(c)), h, ds, c * CHUNK)
    prev, nxt, _, _ = neighbours(pos, jnp.int32(0), jnp.int32(0))
    low = pl.multiple_of(prev * CHUNK + CHUNK - EDGE, EDGE)
    high = pl.multiple_of(nxt * CHUNK, EDGE)
    for h in range(OWN_HEADS):
        for src, dst in ((k, kx), (v, vx)):
            dst[h, 0:EDGE, :] = src[h, pl.ds(low, EDGE), :]
            dst[h, EDGE : EDGE + CHUNK, :] = src[h, 0:CHUNK, :]
            dst[h, EDGE + CHUNK : WIDE, :] = src[h, pl.ds(high, EDGE), :]
        for src, dst in ((q, qx), (ds, dx_)):
            dst[h, 0:EDGE, :] = src[h, pl.ds(low, EDGE), :]
            dst[h, EDGE : 2 * EDGE, :] = src[h, pl.ds(high, EDGE), :]
    low_half, high_half = lax.div(prev, 4), lax.div(nxt, 4)
    low_rows = jnp.where(low_half == 0, stats[place(prev), :, 128:256], stats[place(prev), :, 384:512])
    high_rows = jnp.where(high_half == 0, stats[place(nxt), :, 0:128], stats[place(nxt), :, 256:384])
    low_stats = jnp.transpose(jnp.tile(low_rows, (16, 1)))
    high_stats = jnp.transpose(jnp.tile(high_rows, (16, 1)))
    st[0:EDGE, :] = low_stats[128 - EDGE : 128, :]
    st[EDGE : 2 * EDGE, :] = high_stats[0:EDGE, :]
    for h in range(OWN_HEADS):
        kh = kx[h]
        vh = vx[h]

        def step(dx, carry):
            acc_k, acc_v = carry
            for dz in range(2):
                c = dz * 4 + dx
                at = pl.multiple_of(c * CHUNK, CHUNK)
                qc = q[h, pl.ds(at, CHUNK), :]
                dc = ds[h, pl.ds(at, CHUNK), :]
                row = place(c)
                lanes = slice(dz * CHUNK, (dz + 1) * CHUNK)
                log_total = stats[row, h : h + 1, lanes]
                delta = stats[row, h + OWN_HEADS : h + OWN_HEADS + 1, lanes]
                p = jnp.exp(nt(kh, qc) * SCALE - log_total)
                acc_v = acc_v + nn(p.astype(BF16), dc)
                dsc = (p * (nt(vh, dc) - delta)).astype(BF16)
                acc_k = acc_k + nn(dsc, qc)
            return acc_k, acc_v

        zero = jnp.zeros((WIDE, HEAD_DIM), F32)
        acc_k, acc_v = lax.fori_loop(0, 4, step, (zero, zero))
        p = jnp.exp(nt(qx[h], k[h]) * SCALE - st[:, h : h + 1])
        dsc = (p * (nt(dx_[h], v[h]) - st[:, h + OWN_HEADS : h + OWN_HEADS + 1])).astype(BF16)
        dqx = (nn(dsc, k[h]) * SCALE).astype(BF16)
        cols = slice(h * 128, (h + 1) * 128)
        gs[0:EDGE, cols] = dqx[0:EDGE]
        gs[EDGE : EDGE + CHUNK, cols] = dq[h]
        gs[EDGE + CHUNK : WIDE, cols] = dqx[EDGE : 2 * EDGE]
        gs[:, HALF + h * 128 : HALF + (h + 1) * 128] = (acc_k * SCALE).astype(BF16)
        gs[:, 2 * HALF + h * 128 : 2 * HALF + (h + 1) * 128] = acc_v.astype(BF16)
    mine[...] = gs[pl.ds(pl.multiple_of(core * BLOCK, BLOCK), WINDOW), :]
    give[...] = gs[pl.ds(pl.multiple_of((1 - core) * BLOCK, BLOCK), WINDOW), :]


def conv_body(pos, mine, recv, w_own, w_oth, ext, taps, out, usum, ns, gh, gc):
    _, _, prev_ok, nxt_ok = neighbours(pos, jnp.int32(0), jnp.int32(0))
    first = pos[2] == 0
    low_ok = jnp.where(first, prev_ok, 1.0)
    high_ok = jnp.where(first, 1.0, nxt_ok)
    g = taps[5:6, :]
    for r in range(0, WINDOW, 16):
        ns[r : r + 16, :] = normalize(ext[r : r + 16, :].astype(F32))
    gh[...] = nt(mine[...], w_own[...]) + nt(recv[...], w_oth[...])
    for j in range(0, C, 128):
        tap = [taps[t : t + 1, j : j + 128] for t in range(5)]
        gj = g[:, j : j + 128]
        cols = slice(j, j + 128)

        def grad(r, n):
            near = [ns[r - 2 + t : r - 2 + t + n, cols] for t in range(5)]
            u = tap[0] * (near[0] * gj)
            for t in range(1, 5):
                u = u + tap[t] * (near[t] * gj)
            inner = GELU_ROOT * (u + 0.044715 * u * u * u)
            th = jnp.tanh(inner)
            slope = 0.5 * (1.0 + th) + 0.5 * u * (1.0 - th * th) * GELU_ROOT * (
                1.0 + 3.0 * 0.044715 * u * u
            )
            return near, gh[r : r + n, cols] * slope

        _, edge = grad(8, 8)
        gc[8:16, cols] = edge * low_ok
        _, edge = grad(144, 8)
        gc[144:152, cols] = edge * high_ok
        sums = [jnp.zeros((8, 128), F32) for _ in range(5)]
        for r in range(EDGE, EDGE + BLOCK, 64):
            near, val = grad(r, 64)
            gc[r : r + 64, cols] = val
            for t in range(5):
                sums[t] = sums[t] + jnp.sum((val * near[t]).reshape(8, 8, 128), axis=0)
        side, slot = divmod(j // 128, OWN_HEADS)
        for t in range(5):
            row = t * OWN_HEADS + slot
            usum[side, row : row + 1, :] = jnp.sum(sums[t], axis=0, keepdims=True)
    usum[:, 15:16, :] = jnp.zeros((2, 1, 128), F32)
    tap = [taps[t : t + 1, :] for t in range(5)]
    for r in range(EDGE, EDGE + BLOCK, 16):
        gn = tap[0] * gc[r + 2 : r + 18, :]
        for t in range(1, 5):
            gn = gn + tap[t] * gc[r + 2 - t : r + 18 - t, :]
        x = ext[r : r + 16, :].astype(F32)
        inv = lax.rsqrt(jnp.mean(x * x, axis=-1, keepdims=True) + EPSILON)
        scaled = gn * g
        inner = jnp.mean(scaled * x, axis=-1, keepdims=True)
        res = gh[r : r + 16, :] + inv * scaled - x * (inv * inv * inv * inner)
        out[r - EDGE : r - EDGE + 16, :] = res.astype(BF16)


AXES = ("y", "zm", "zl", "zh", "x", "core")


def swap(a, axis):
    return lax.ppermute(a, axis, [(0, 1), (1, 0)])


def from_x(a, step):
    return lax.ppermute(a, "x", [((i + step) % 4, i) for i in range(4)])


def share(a, axes, size):
    wide = jnp.broadcast_to(a[None], (size,) + a.shape)
    return lax.all_to_all(wide, axes, 0, 0)


def shards(signal, norm_gain, conv_taps, w_query, w_key, w_value, cotangent):
    zh = lax.axis_index("zh")
    xi = lax.axis_index("x")
    core = lax.axis_index("core")
    pos = jnp.stack([zh, xi, core]).astype(jnp.int32)
    first = core == 0
    sig = signal[0]
    cot = cotangent[0]
    gain = norm_gain.reshape(1, C)

    def halves(a):
        low, high = a[:, :HALF], a[:, HALF:]
        return jnp.where(first, low, high), jnp.where(first, high, low)

    both = jnp.concatenate([sig, cot], axis=0)
    both_z = swap(both, "zh")
    near = share(both, "x", 4)

    def exchange(a):
        rows, cots = a[:, :BLOCK], a[:, BLOCK:]
        give = jnp.where(first, cots[:, :, HALF:], cots[:, :, :HALF])
        return swap(jnp.concatenate([rows, give], axis=-1), "core")

    parts = [halves(w) for w in (w_query, w_key, w_value)]
    w_own = jnp.concatenate([p[0] for p in parts], axis=1)
    w_oth = jnp.concatenate([p[1] for p in parts], axis=1)
    coef = jnp.concatenate([conv_taps, gain, jnp.zeros((2, C), F32)], axis=0)
    both_z, near, w_own, w_oth, coef = lax.optimization_barrier(
        (both_z, near, w_own, w_oth, coef)
    )
    e0 = exchange(near)
    far = share(both_z, "x", 4)
    e1 = exchange(far)

    head_shape = jax.ShapeDtypeStruct((OWN_HEADS, BINS, HEAD_DIM), BF16)
    q, k, v, ext = call(
        hidden_body,
        (head_shape, head_shape, head_shape, jax.ShapeDtypeStruct((160, C), BF16)),
        (pos, near, far, e0, e1, w_own, coef),
        (VM((CHUNKS, CHUNK, C), BF16), VM((288, C), F32), VM((CHUNK, C), BF16)),
    )
    part = jax.ShapeDtypeStruct((OWN_HEADS, CHUNK, HEAD_DIM), BF16)
    dq, stats = call(
        forward_body,
        (part, jax.ShapeDtypeStruct((8, 2 * CHUNK), F32)),
        (pos, q, k, v, near, far, e0, e1),
        (
            VM((OWN_HEADS, 2 * CHUNK, HEAD_DIM), BF16),
            VM((CHUNK, BINS), F32),
            VM((2 * CHUNK, 128), F32),
        ),
    )
    stats_all = share(stats, "x", 4)
    grads = jax.ShapeDtypeStruct((WINDOW, 3 * HALF), BF16)
    mine, give = call(
        backward_body,
        (grads, grads),
        (pos, q, k, v, dq, near, far, e0, e1, stats_all),
        (
            VM((OWN_HEADS, BINS, HEAD_DIM), BF16),
            VM((WIDE, 3 * HALF), BF16),
            VM((OWN_HEADS, WIDE, HEAD_DIM), BF16),
            VM((OWN_HEADS, WIDE, HEAD_DIM), BF16),
            VM((OWN_HEADS, 2 * EDGE, HEAD_DIM), BF16),
            VM((OWN_HEADS, 2 * EDGE, HEAD_DIM), BF16),
            VM((2 * EDGE, 128), F32),
        ),
    )
    recv = swap(give, "core")
    out, usum = call(
        conv_body,
        (jax.ShapeDtypeStruct((BLOCK, C), BF16), jax.ShapeDtypeStruct((2, 16, 128), F32)),
        (pos, mine, recv, w_own, w_oth, ext, coef),
        (VM((WINDOW, C), F32), VM((WINDOW, C), F32), VM((WINDOW, C), F32)),
    )
    wide = jnp.broadcast_to(usum[None], (16, 2, 16, 128)).reshape(32, 16, 128)
    part = jnp.sum(lax.all_to_all(wide, ("y", "x", "core"), 0, 0), axis=0)
    part = share(part.astype(BF16), ("zm", "zl", "zh"), 16).astype(F32)
    part = jnp.sum(part, axis=0)
    usum = lax.all_gather(part, "core", axis=0)[:, :15].reshape(2, 5, HALF)
    usum = jnp.concatenate([usum[0], usum[1]], axis=1)
    grad_taps = usum * gain
    grad_gain = jnp.sum(usum * conv_taps, axis=0)
    return out[None], grad_taps, grad_gain


def solution(mesh):
    shape = (mesh.devices.size // 128, 2, 4, 2, 4, 2)
    fine = Mesh(mesh.devices.reshape(shape), AXES)
    rows = P(("y", "zm", "zl"), ("zh", "x", "core"), None)
    in_specs = (rows, P(), P(), P(), P(), P(), rows)
    out_specs = (rows, P(), P())
    return jax.shard_map(shards, mesh=fine, in_specs=in_specs, out_specs=out_specs, check_vma=False)
```

```python
import math

import jax
import jax.numpy as jnp
from jax import lax
from jax.experimental import pallas as pl
from jax.experimental.pallas import tpu as pltpu
from jax.sharding import Mesh
from jax.sharding import PartitionSpec as P

HEADS = 6
HEAD_DIM = 128
OWN_HEADS = 3
HALF = OWN_HEADS * HEAD_DIM
EPSILON = 1e-06
GELU_ROOT = math.sqrt(2.0 / math.pi)
SCALE = 1.0 / math.sqrt(HEAD_DIM)
LOG2E = math.log2(math.e)
BLOCK = 128
CHUNK = 256
CHUNKS = 8
BINS = 2048
C = 768
INTERPRET = False
F32 = jnp.float32
BF16 = jnp.bfloat16
VM = pltpu.VMEM


def vspec():
    return pl.BlockSpec(memory_space=pltpu.VMEM)


def sspec():
    return pl.BlockSpec(memory_space=pltpu.SMEM)


def call(body, out_shape, args, scratch=(), limit=16):
    specs = [sspec() if a.dtype == jnp.int32 else vspec() for a in args]
    outs = jax.tree.map(lambda _: vspec(), out_shape)
    return pl.pallas_call(
        body,
        out_shape=out_shape,
        in_specs=specs,
        out_specs=outs,
        scratch_shapes=list(scratch),
        compiler_params=pltpu.CompilerParams(vmem_limit_bytes=limit << 20),
        interpret=INTERPRET,
    )(*args)


def nt(a, b):
    return lax.dot_general(a, b, (((1,), (1,)), ((), ())), preferred_element_type=F32)


def nn(a, b):
    return lax.dot_general(a, b, (((1,), (0,)), ((), ())), preferred_element_type=F32)


def neighbours(pos, dz, dx):
    zh = pos[0]
    xa = lax.rem(pos[1] + dx, 4)
    za = lax.rem(zh + dz, 2)
    wrap_lo = (xa == 0).astype(jnp.int32)
    wrap_hi = (xa == 3).astype(jnp.int32)
    prev = lax.rem(dz + wrap_lo, 2) * 4 + lax.rem(dx + 3, 4)
    nxt = lax.rem(dz + wrap_hi, 2) * 4 + lax.rem(dx + 1, 4)
    prev_ok = 1 - wrap_lo * (1 - za)
    nxt_ok = 1 - wrap_hi * za
    return prev, nxt, prev_ok.astype(F32), nxt_ok.astype(F32)


def normalize(rows):
    return rows * lax.rsqrt(jnp.mean(rows * rows, axis=-1, keepdims=True) + EPSILON)


def hidden_body(
    pos, near, other, w, taps, q, k, v, ext, xs, ns, hs, ns2, hs2
):
    core = pos[2]
    here = pl.multiple_of(core * BLOCK, BLOCK)
    there = pl.multiple_of((1 - core) * BLOCK, BLOCK)
    for c in range(CHUNKS):
        xa = lax.rem(pos[1] + c % 4, 4)
        sl = slice((c // 4) * BLOCK, (c // 4 + 1) * BLOCK)
        xs[c, pl.ds(here, BLOCK), :] = near[xa, sl, :]
        xs[c, pl.ds(there, BLOCK), :] = other[xa, sl, :]
    prev, nxt, prev_ok, nxt_ok = neighbours(pos, jnp.int32(0), jnp.int32(0))
    first = core == 0
    ext[16:144, :] = near[pos[1], 0:BLOCK, :]

    @pl.when(first)
    def _():
        ext[0:16, :] = (xs[prev, 240:256, :].astype(F32) * prev_ok).astype(BF16)
        ext[144:160, :] = xs[0, 128:144, :]

    @pl.when(jnp.logical_not(first))
    def _():
        ext[0:16, :] = xs[0, 112:128, :]
        ext[144:160, :] = (xs[nxt, 0:16, :].astype(F32) * nxt_ok).astype(BF16)

    def prepare(c, ns, hs):
        dz = lax.div(c, 4)
        dx = lax.rem(c, 4)
        prev, nxt, prev_ok, nxt_ok = neighbours(pos, dz, dx)
        g = taps[5:6, :]
        ns[0:16, :] = normalize(xs[prev, 240:256, :].astype(F32)) * g * prev_ok
        ns[272:288, :] = normalize(xs[nxt, 0:16, :].astype(F32)) * g * nxt_ok
        for r in range(0, CHUNK, 16):
            ns[16 + r : 32 + r, :] = normalize(xs[c, r : r + 16, :].astype(F32)) * g
        for j in range(0, C, 128):
            tap = [taps[t : t + 1, j : j + 128] for t in range(5)]
            for r in range(0, CHUNK, 64):
                u = tap[0] * ns[14 + r : 78 + r, j : j + 128]
                for t in range(1, 5):
                    u = u + tap[t] * ns[14 + r + t : 78 + r + t, j : j + 128]
                inner = u * (GELU_ROOT + (GELU_ROOT * 0.044715) * (u * u))
                half = 0.5 * u
                x = xs[c, r : r + 64, j : j + 128].astype(F32)
                hs[r : r + 64, j : j + 128] = (x + (half + half * jnp.tanh(inner))).astype(BF16)

    def project(c, hs):
        y = nn(hs[...], w[...]).astype(BF16)
        at = pl.multiple_of(c * CHUNK, CHUNK)
        for h in range(OWN_HEADS):
            q[h, pl.ds(at, CHUNK), :] = y[:, h * 128 : (h + 1) * 128]
            k[h, pl.ds(at, CHUNK), :] = y[:, HALF + h * 128 : HALF + (h + 1) * 128]
            v[h, pl.ds(at, CHUNK), :] = y[:, 2 * HALF + h * 128 : 2 * HALF + (h + 1) * 128]

    prepare(jnp.int32(0), ns, hs)

    def pair(i, _):
        c = 2 * i
        project(c, hs)
        prepare(c + 1, ns2, hs2)
        project(c + 1, hs2)
        prepare(c + 2, ns, hs)
        return 0

    lax.fori_loop(0, CHUNKS // 2 - 1, pair, 0)
    project(jnp.int32(CHUNKS - 2), hs)
    prepare(jnp.int32(CHUNKS - 1), ns2, hs2)
    project(jnp.int32(CHUNKS - 1), hs2)


HID_SCRATCH = (
    VM((CHUNKS, CHUNK, C), BF16),
    VM((288, C), F32),
    VM((CHUNK, C), BF16),
    VM((288, C), F32),
    VM((CHUNK, C), BF16),
)


KB = 512


def forward_body(q, k, v, d0, d4, dq, stats, ds, ss, sm):
    for g, d in enumerate((d0, d4)):
        for h in range(OWN_HEADS):
            ds[h, g * CHUNK : g * CHUNK + BLOCK, :] = d[0:BLOCK, h * 128 : (h + 1) * 128]
            ds[h, g * CHUNK + BLOCK : (g + 1) * CHUNK, :] = d[
                0:BLOCK, HALF + h * 128 : HALF + (h + 1) * 128
            ]
    sm[...] = jnp.zeros_like(sm)
    lane = lax.broadcasted_iota(jnp.int32, (CHUNK, 128), 1)

    def head(h, _):
        for g in range(2):
            qh = q[h, g * 1024 : g * 1024 + CHUNK, :]
            top = None
            for b in range(0, BINS, KB):
                s = nt(qh, k[h, b : b + KB, :])
                ss[g, :, b : b + KB] = s
                m = jnp.max(s, axis=1, keepdims=True)
                top = m if top is None else jnp.maximum(top, m)
            total = jnp.zeros((CHUNK, 1), F32)
            out = jnp.zeros((CHUNK, HEAD_DIM), F32)
            for b in range(0, BINS, KB):
                p = jnp.exp2((ss[g, :, b : b + KB] - top) * (SCALE * LOG2E))
                total = total + jnp.sum(p, axis=1, keepdims=True)
                out = out + nn(p.astype(BF16), v[h, b : b + KB, :])
                if g == 0:
                    ss[g, :, b : b + KB] = p
            inverse = 1.0 / total
            attended = (out * inverse).astype(BF16).astype(F32)
            do = ds[h, g * CHUNK : (g + 1) * CHUNK, :]
            delta = jnp.sum(do.astype(F32) * attended, axis=1, keepdims=True)
            log_total = top * SCALE + jnp.log(total)
            sl = slice(g * CHUNK, (g + 1) * CHUNK)
            sm[sl, :] = jnp.where(
                lane == h, log_total, jnp.where(lane == h + OWN_HEADS, delta, sm[sl, :])
            )
            if g == 0:
                acc = jnp.zeros((CHUNK, HEAD_DIM), F32)
                for b in range(0, BINS, KB):
                    dp = nt(do, v[h, b : b + KB, :])
                    dsc = (ss[g, :, b : b + KB] * (dp - delta)).astype(BF16)
                    acc = acc + nn(dsc, k[h, b : b + KB, :])
                dq[h, :, :] = (acc * (inverse * SCALE)).astype(BF16)
        return 0

    for h in range(OWN_HEADS):
        head(h, 0)
    stats[...] = jnp.transpose(sm[...])[0:8, :]


FWD_SCRATCH = (VM((OWN_HEADS, 2 * CHUNK, HEAD_DIM), BF16), VM((2, CHUNK, BINS), F32), VM((2 * CHUNK, 128), F32))

EDGE = 16
WIDE = CHUNK + 2 * EDGE
WINDOW = BLOCK + 2 * EDGE


def backward_body(
    pos, q, k, v, dq, d0, d4, b1, b2, b3, stats, mine, give, ds, gs, kx, vx, qx, dx_, st
):
    core = pos[2]

    def place(c):
        return lax.rem(pos[1] + c, 4)

    blocks = ((d0, 0), (b1, 0), (b2, 0), (b3, 0), (d4, 0), (b1, BLOCK), (b2, BLOCK), (b3, BLOCK))
    for c, (d, low) in enumerate(blocks):
        for h in range(OWN_HEADS):
            lo = c * CHUNK
            rows = slice(low, low + BLOCK)
            ds[h, lo : lo + BLOCK, :] = d[rows, h * 128 : (h + 1) * 128]
            ds[h, lo + BLOCK : lo + CHUNK, :] = d[rows, HALF + h * 128 : HALF + (h + 1) * 128]
    prev, nxt, _, _ = neighbours(pos, jnp.int32(0), jnp.int32(0))
    low = pl.multiple_of(prev * CHUNK + CHUNK - EDGE, EDGE)
    high = pl.multiple_of(nxt * CHUNK, EDGE)
    for h in range(OWN_HEADS):
        for src, dst in ((k, kx), (v, vx)):
            dst[h, 0:EDGE, :] = src[h, pl.ds(low, EDGE), :]
            dst[h, EDGE : EDGE + CHUNK, :] = src[h, 0:CHUNK, :]
            dst[h, EDGE + CHUNK : WIDE, :] = src[h, pl.ds(high, EDGE), :]
        for src, dst in ((q, qx), (ds, dx_)):
            dst[h, 0:EDGE, :] = src[h, pl.ds(low, EDGE), :]
            dst[h, EDGE : 2 * EDGE, :] = src[h, pl.ds(high, EDGE), :]
    low_half, high_half = lax.div(prev, 4), lax.div(nxt, 4)
    low_rows = jnp.where(low_half == 0, stats[place(prev), :, 128:256], stats[place(prev), :, 384:512])
    high_rows = jnp.where(high_half == 0, stats[place(nxt), :, 0:128], stats[place(nxt), :, 256:384])
    low_stats = jnp.transpose(jnp.tile(low_rows, (16, 1)))
    high_stats = jnp.transpose(jnp.tile(high_rows, (16, 1)))
    st[0:EDGE, :] = low_stats[128 - EDGE : 128, :]
    st[EDGE : 2 * EDGE, :] = high_stats[0:EDGE, :]
    def step(dx, carry):
        row = place(dx)
        res = []
        for h in range(OWN_HEADS):
            acc_k, acc_v = carry[2 * h], carry[2 * h + 1]
            for dz in range(2):
                at = pl.multiple_of((dz * 4 + dx) * CHUNK, CHUNK)
                qc = q[h, pl.ds(at, CHUNK), :]
                dc = ds[h, pl.ds(at, CHUNK), :]
                lanes = slice(dz * CHUNK, (dz + 1) * CHUNK)
                log_total = stats[row, h : h + 1, lanes]
                delta = stats[row, h + OWN_HEADS : h + OWN_HEADS + 1, lanes]
                p = jnp.exp2(nt(kx[h], qc) * (SCALE * LOG2E) - log_total * LOG2E)
                acc_v = acc_v + nn(p.astype(BF16), dc)
                dsc = (p * (nt(vx[h], dc) - delta)).astype(BF16)
                acc_k = acc_k + nn(dsc, qc)
            res += [acc_k, acc_v]
        return tuple(res)

    zero = jnp.zeros((WIDE, HEAD_DIM), F32)
    sums = lax.fori_loop(0, 4, step, (zero,) * 6)
    for h in range(OWN_HEADS):
        acc_k, acc_v = sums[2 * h], sums[2 * h + 1]
        p = jnp.exp(nt(qx[h], k[h]) * SCALE - st[:, h : h + 1])
        dsc = (p * (nt(dx_[h], v[h]) - st[:, h + OWN_HEADS : h + OWN_HEADS + 1])).astype(BF16)
        dqx = (nn(dsc, k[h]) * SCALE).astype(BF16)
        cols = slice(h * 128, (h + 1) * 128)
        gs[0:EDGE, cols] = dqx[0:EDGE]
        gs[EDGE : EDGE + CHUNK, cols] = dq[h]
        gs[EDGE + CHUNK : WIDE, cols] = dqx[EDGE : 2 * EDGE]
        gs[:, HALF + h * 128 : HALF + (h + 1) * 128] = (acc_k * SCALE).astype(BF16)
        gs[:, 2 * HALF + h * 128 : 2 * HALF + (h + 1) * 128] = acc_v.astype(BF16)
    mine[...] = gs[pl.ds(pl.multiple_of(core * BLOCK, BLOCK), WINDOW), :]
    give[...] = gs[pl.ds(pl.multiple_of((1 - core) * BLOCK, BLOCK), WINDOW), :]


def conv_body(pos, mine, recv, w_own, w_oth, ext, taps, out, usum, ns, gh, gc):
    _, _, prev_ok, nxt_ok = neighbours(pos, jnp.int32(0), jnp.int32(0))
    first = pos[2] == 0
    low_ok = jnp.where(first, prev_ok, 1.0)
    high_ok = jnp.where(first, 1.0, nxt_ok)
    g = taps[5:6, :]
    for r in range(0, WINDOW, 16):
        ns[r : r + 16, :] = normalize(ext[r : r + 16, :].astype(F32))
    gh[...] = nt(mine[...], w_own[...]) + nt(recv[...], w_oth[...])
    for j in range(0, C, 128):
        tap = [taps[t : t + 1, j : j + 128] for t in range(5)]
        gj = g[:, j : j + 128]
        cols = slice(j, j + 128)

        def grad(r, n):
            near = [ns[r - 2 + t : r - 2 + t + n, cols] for t in range(5)]
            u = tap[0] * (near[0] * gj)
            for t in range(1, 5):
                u = u + tap[t] * (near[t] * gj)
            inner = GELU_ROOT * (u + 0.044715 * u * u * u)
            th = jnp.tanh(inner)
            slope = 0.5 * (1.0 + th) + 0.5 * u * (1.0 - th * th) * GELU_ROOT * (
                1.0 + 3.0 * 0.044715 * u * u
            )
            return near, gh[r : r + n, cols] * slope

        _, edge = grad(8, 8)
        gc[8:16, cols] = edge * low_ok
        _, edge = grad(144, 8)
        gc[144:152, cols] = edge * high_ok
        sums = [jnp.zeros((8, 128), F32) for _ in range(5)]
        for r in range(EDGE, EDGE + BLOCK, 64):
            near, val = grad(r, 64)
            gc[r : r + 64, cols] = val
            for t in range(5):
                sums[t] = sums[t] + jnp.sum((val * near[t]).reshape(8, 8, 128), axis=0)
        side, slot = divmod(j // 128, OWN_HEADS)
        for t in range(5):
            row = t * OWN_HEADS + slot
            usum[side, row : row + 1, :] = jnp.sum(sums[t], axis=0, keepdims=True)
    usum[:, 15:16, :] = jnp.zeros((2, 1, 128), F32)
    tap = [taps[t : t + 1, :] for t in range(5)]
    for r in range(EDGE, EDGE + BLOCK, 16):
        gn = tap[0] * gc[r + 2 : r + 18, :]
        for t in range(1, 5):
            gn = gn + tap[t] * gc[r + 2 - t : r + 18 - t, :]
        x = ext[r : r + 16, :].astype(F32)
        inv = lax.rsqrt(jnp.mean(x * x, axis=-1, keepdims=True) + EPSILON)
        scaled = gn * g
        inner = jnp.mean(scaled * x, axis=-1, keepdims=True)
        res = gh[r : r + 16, :] + inv * scaled - x * (inv * inv * inv * inner)
        out[r - EDGE : r - EDGE + 16, :] = res.astype(BF16)


AXES = ("y", "zm", "zl", "zh", "x", "core")


def swap(a, axis):
    return lax.ppermute(a, axis, [(0, 1), (1, 0)])


def from_x(a, step):
    return lax.ppermute(a, "x", [((i + step) % 4, i) for i in range(4)])


def share(a, axes, size):
    wide = jnp.broadcast_to(a[None], (size,) + a.shape)
    return lax.all_to_all(wide, axes, 0, 0)


def shards(signal, norm_gain, conv_taps, w_query, w_key, w_value, cotangent):
    zh = lax.axis_index("zh")
    xi = lax.axis_index("x")
    core = lax.axis_index("core")
    pos = jnp.stack([zh, xi, core]).astype(jnp.int32)
    first = core == 0
    sig = signal[0]
    cot = cotangent[0]
    gain = norm_gain.reshape(1, C)

    def halves(a):
        low, high = a[:, :HALF], a[:, HALF:]
        return jnp.where(first, low, high), jnp.where(first, high, low)

    keep, give = halves(cot)
    got = swap(give, "core")
    cot_own = jnp.concatenate(
        [jnp.where(first, keep, got), jnp.where(first, got, keep)], axis=1
    )
    sig_z = swap(sig, "zh")
    parts = [halves(w) for w in (w_query, w_key, w_value)]
    w_own = jnp.concatenate([p[0] for p in parts], axis=1)
    w_oth = jnp.concatenate([p[1] for p in parts], axis=1)
    coef = jnp.concatenate([conv_taps, gain, jnp.zeros((2, C), F32)], axis=0)
    sig_z, cot_own, w_own, w_oth, coef = lax.optimization_barrier(
        (sig_z, cot_own, w_own, w_oth, coef)
    )
    cot_z = swap(cot_own, "zh")
    near = share(jnp.concatenate([sig, sig_z], axis=0), "x", 4)
    near, cot_z = lax.optimization_barrier((near, cot_z))
    other = swap(near, "core")
    both = jnp.concatenate([cot_own, cot_z], axis=0)
    cots = [from_x(both, d) for d in (1, 2, 3)]

    head_shape = jax.ShapeDtypeStruct((OWN_HEADS, BINS, HEAD_DIM), BF16)
    q, k, v, ext = call(
        hidden_body,
        (head_shape, head_shape, head_shape, jax.ShapeDtypeStruct((160, C), BF16)),
        (pos, near, other, w_own, coef),
        HID_SCRATCH,
    )
    part = jax.ShapeDtypeStruct((OWN_HEADS, CHUNK, HEAD_DIM), BF16)
    dq, stats = call(
        forward_body,
        (part, jax.ShapeDtypeStruct((8, 2 * CHUNK), F32)),
        (q, k, v, cot_own, cot_z),
        FWD_SCRATCH,
    )
    stats, cots = lax.optimization_barrier((stats, cots))
    stats_all = share(stats, "x", 4)
    grads = jax.ShapeDtypeStruct((WINDOW, 3 * HALF), BF16)
    mine, give = call(
        backward_body,
        (grads, grads),
        (pos, q, k, v, dq, cot_own, cot_z, *cots, stats_all),
        (
            VM((OWN_HEADS, BINS, HEAD_DIM), BF16),
            VM((WIDE, 3 * HALF), BF16),
            VM((OWN_HEADS, WIDE, HEAD_DIM), BF16),
            VM((OWN_HEADS, WIDE, HEAD_DIM), BF16),
            VM((OWN_HEADS, 2 * EDGE, HEAD_DIM), BF16),
            VM((OWN_HEADS, 2 * EDGE, HEAD_DIM), BF16),
            VM((2 * EDGE, 128), F32),
        ),
    )
    recv = swap(give, "core")
    out, usum = call(
        conv_body,
        (jax.ShapeDtypeStruct((BLOCK, C), BF16), jax.ShapeDtypeStruct((2, 16, 128), F32)),
        (pos, mine, recv, w_own, w_oth, ext, coef),
        (VM((WINDOW, C), F32), VM((WINDOW, C), F32), VM((WINDOW, C), F32)),
    )
    wide = jnp.broadcast_to(usum[None], (16, 2, 16, 128)).reshape(32, 16, 128)
    part = jnp.sum(lax.all_to_all(wide, ("y", "x", "core"), 0, 0), axis=0)
    part = share(part.astype(BF16), ("zm", "zl", "zh"), 16).astype(F32)
    part = jnp.sum(part, axis=0)
    usum = lax.all_gather(part, "core", axis=0)[:, :15].reshape(2, 5, HALF)
    usum = jnp.concatenate([usum[0], usum[1]], axis=1)
    grad_taps = usum * gain
    grad_gain = jnp.sum(usum * conv_taps, axis=0)
    return out[None], grad_taps, grad_gain


def solution(mesh):
    shape = (mesh.devices.size // 128, 2, 4, 2, 4, 2)
    fine = Mesh(mesh.devices.reshape(shape), AXES)
    rows = P(("y", "zm", "zl"), ("zh", "x", "core"), None)
    in_specs = (rows, P(), P(), P(), P(), P(), rows)
    out_specs = (rows, P(), P())
    return jax.shard_map(shards, mesh=fine, in_specs=in_specs, out_specs=out_specs, check_vma=False)
```

```python
import math

import jax
import jax.numpy as jnp
from jax import lax
from jax.experimental import pallas as pl
from jax.experimental.pallas import tpu as pltpu
from jax.sharding import Mesh
from jax.sharding import PartitionSpec as P

HEADS = 6
HEAD_DIM = 128
OWN_HEADS = 3
HALF = OWN_HEADS * HEAD_DIM
EPSILON = 1e-06
GELU_ROOT = math.sqrt(2.0 / math.pi)
SCALE = 1.0 / math.sqrt(HEAD_DIM)
LOG2E = math.log2(math.e)
BLOCK = 128
CHUNK = 256
CHUNKS = 8
BINS = 2048
C = 768
INTERPRET = False
F32 = jnp.float32
BF16 = jnp.bfloat16
VM = pltpu.VMEM


def vspec():
    return pl.BlockSpec(memory_space=pltpu.VMEM)


def sspec():
    return pl.BlockSpec(memory_space=pltpu.SMEM)


def call(body, out_shape, args, scratch=(), limit=16):
    specs = [sspec() if a.dtype == jnp.int32 else vspec() for a in args]
    outs = jax.tree.map(lambda _: vspec(), out_shape)
    return pl.pallas_call(
        body,
        out_shape=out_shape,
        in_specs=specs,
        out_specs=outs,
        scratch_shapes=list(scratch),
        compiler_params=pltpu.CompilerParams(vmem_limit_bytes=limit << 20),
        interpret=INTERPRET,
    )(*args)


def nt(a, b):
    return lax.dot_general(a, b, (((1,), (1,)), ((), ())), preferred_element_type=F32)


def nn(a, b):
    return lax.dot_general(a, b, (((1,), (0,)), ((), ())), preferred_element_type=F32)


def neighbours(pos, dz, dx):
    zh = pos[0]
    xa = lax.rem(pos[1] + dx, 4)
    za = lax.rem(zh + dz, 2)
    wrap_lo = (xa == 0).astype(jnp.int32)
    wrap_hi = (xa == 3).astype(jnp.int32)
    prev = lax.rem(dz + wrap_lo, 2) * 4 + lax.rem(dx + 3, 4)
    nxt = lax.rem(dz + wrap_hi, 2) * 4 + lax.rem(dx + 1, 4)
    prev_ok = 1 - wrap_lo * (1 - za)
    nxt_ok = 1 - wrap_hi * za
    return prev, nxt, prev_ok.astype(F32), nxt_ok.astype(F32)


def normalize(rows):
    return rows * lax.rsqrt(jnp.mean(rows * rows, axis=-1, keepdims=True) + EPSILON)


def hidden_body(
    pos, near, other, w, taps, q, k, v, ext, xs, ns, hs, ns2, hs2
):
    core = pos[2]
    here = pl.multiple_of(core * BLOCK, BLOCK)
    there = pl.multiple_of((1 - core) * BLOCK, BLOCK)
    for c in range(CHUNKS):
        xa = lax.rem(pos[1] + c % 4, 4)
        sl = slice((c // 4) * BLOCK, (c // 4 + 1) * BLOCK)
        xs[c, pl.ds(here, BLOCK), :] = near[xa, sl, :]
        xs[c, pl.ds(there, BLOCK), :] = other[xa, sl, :]
    prev, nxt, prev_ok, nxt_ok = neighbours(pos, jnp.int32(0), jnp.int32(0))
    first = core == 0
    ext[16:144, :] = near[pos[1], 0:BLOCK, :]

    @pl.when(first)
    def _():
        ext[0:16, :] = (xs[prev, 240:256, :].astype(F32) * prev_ok).astype(BF16)
        ext[144:160, :] = xs[0, 128:144, :]

    @pl.when(jnp.logical_not(first))
    def _():
        ext[0:16, :] = xs[0, 112:128, :]
        ext[144:160, :] = (xs[nxt, 0:16, :].astype(F32) * nxt_ok).astype(BF16)

    def prepare(c, ns, hs):
        dz = lax.div(c, 4)
        dx = lax.rem(c, 4)
        prev, nxt, prev_ok, nxt_ok = neighbours(pos, dz, dx)
        g = taps[5:6, :]
        ns[0:16, :] = normalize(xs[prev, 240:256, :].astype(F32)) * g * prev_ok
        ns[272:288, :] = normalize(xs[nxt, 0:16, :].astype(F32)) * g * nxt_ok
        for r in range(0, CHUNK, 16):
            ns[16 + r : 32 + r, :] = normalize(xs[c, r : r + 16, :].astype(F32)) * g
        for j in range(0, C, 128):
            tap = [taps[t : t + 1, j : j + 128] for t in range(5)]
            for r in range(0, CHUNK, 64):
                u = tap[0] * ns[14 + r : 78 + r, j : j + 128]
                for t in range(1, 5):
                    u = u + tap[t] * ns[14 + r + t : 78 + r + t, j : j + 128]
                inner = u * (GELU_ROOT + (GELU_ROOT * 0.044715) * (u * u))
                half = 0.5 * u
                x = xs[c, r : r + 64, j : j + 128].astype(F32)
                hs[r : r + 64, j : j + 128] = (x + (half + half * jnp.tanh(inner))).astype(BF16)

    def project(c, hs):
        y = nn(hs[...], w[...]).astype(BF16)
        at = pl.multiple_of(c * CHUNK, CHUNK)
        for h in range(OWN_HEADS):
            q[h, pl.ds(at, CHUNK), :] = y[:, h * 128 : (h + 1) * 128]
            k[h, pl.ds(at, CHUNK), :] = y[:, HALF + h * 128 : HALF + (h + 1) * 128]
            v[h, pl.ds(at, CHUNK), :] = y[:, 2 * HALF + h * 128 : 2 * HALF + (h + 1) * 128]

    prepare(jnp.int32(0), ns, hs)

    def pair(i, _):
        c = 2 * i
        project(c, hs)
        prepare(c + 1, ns2, hs2)
        project(c + 1, hs2)
        prepare(c + 2, ns, hs)
        return 0

    lax.fori_loop(0, CHUNKS // 2 - 1, pair, 0)
    project(jnp.int32(CHUNKS - 2), hs)
    prepare(jnp.int32(CHUNKS - 1), ns2, hs2)
    project(jnp.int32(CHUNKS - 1), hs2)


HID_SCRATCH = (
    VM((CHUNKS, CHUNK, C), BF16),
    VM((288, C), F32),
    VM((CHUNK, C), BF16),
    VM((288, C), F32),
    VM((CHUNK, C), BF16),
)


KB = 512


def forward_body(q, k, v, d0, d4, dq, stats, ds, ss, sm):
    for g, d in enumerate((d0, d4)):
        for h in range(OWN_HEADS):
            ds[h, g * CHUNK : g * CHUNK + BLOCK, :] = d[0:BLOCK, h * 128 : (h + 1) * 128]
            ds[h, g * CHUNK + BLOCK : (g + 1) * CHUNK, :] = d[
                0:BLOCK, HALF + h * 128 : HALF + (h + 1) * 128
            ]
    sm[...] = jnp.zeros_like(sm)
    lane = lax.broadcasted_iota(jnp.int32, (CHUNK, 128), 1)

    def head(h, _):
        for g in range(2):
            qh = q[h, g * 1024 : g * 1024 + CHUNK, :]
            top = None
            for b in range(0, BINS, KB):
                s = nt(qh, k[h, b : b + KB, :])
                ss[g, :, b : b + KB] = s
                m = jnp.max(s, axis=1, keepdims=True)
                top = m if top is None else jnp.maximum(top, m)
            total = jnp.zeros((CHUNK, 1), F32)
            out = jnp.zeros((CHUNK, HEAD_DIM), F32)
            for b in range(0, BINS, KB):
                p = jnp.exp2((ss[g, :, b : b + KB] - top) * (SCALE * LOG2E))
                total = total + jnp.sum(p, axis=1, keepdims=True)
                out = out + nn(p.astype(BF16), v[h, b : b + KB, :])
                if g == 0:
                    ss[g, :, b : b + KB] = p
            inverse = 1.0 / total
            attended = (out * inverse).astype(BF16).astype(F32)
            do = ds[h, g * CHUNK : (g + 1) * CHUNK, :]
            delta = jnp.sum(do.astype(F32) * attended, axis=1, keepdims=True)
            log_total = top * SCALE + jnp.log(total)
            sl = slice(g * CHUNK, (g + 1) * CHUNK)
            sm[sl, :] = jnp.where(
                lane == h, log_total, jnp.where(lane == h + OWN_HEADS, delta, sm[sl, :])
            )
            if g == 0:
                acc = jnp.zeros((CHUNK, HEAD_DIM), F32)
                for b in range(0, BINS, KB):
                    dp = nt(do, v[h, b : b + KB, :])
                    dsc = (ss[g, :, b : b + KB] * (dp - delta)).astype(BF16)
                    acc = acc + nn(dsc, k[h, b : b + KB, :])
                dq[h, :, :] = (acc * (inverse * SCALE)).astype(BF16)
        return 0

    for h in range(OWN_HEADS):
        head(h, 0)
    stats[...] = jnp.transpose(sm[...])[0:8, :]


FWD_SCRATCH = (VM((OWN_HEADS, 2 * CHUNK, HEAD_DIM), BF16), VM((2, CHUNK, BINS), F32), VM((2 * CHUNK, 128), F32))

EDGE = 16
WIDE = CHUNK + 2 * EDGE
WINDOW = BLOCK + 2 * EDGE


def backward_body(
    pos, q, k, v, dq, d0, d4, d1, d2, d3, d5, d6, d7, stats, mine, give, ds, gs, kx, vx, qx, dx_, st
):
    core = pos[2]

    def place(c):
        return lax.rem(pos[1] + c, 4)

    for c, d in enumerate((d0, d1, d2, d3, d4, d5, d6, d7)):
        for h in range(OWN_HEADS):
            lo = c * CHUNK
            rows = slice(0, BLOCK)
            ds[h, lo : lo + BLOCK, :] = d[rows, h * 128 : (h + 1) * 128]
            ds[h, lo + BLOCK : lo + CHUNK, :] = d[rows, HALF + h * 128 : HALF + (h + 1) * 128]
    prev, nxt, _, _ = neighbours(pos, jnp.int32(0), jnp.int32(0))
    low = pl.multiple_of(prev * CHUNK + CHUNK - EDGE, EDGE)
    high = pl.multiple_of(nxt * CHUNK, EDGE)
    for h in range(OWN_HEADS):
        for src, dst in ((k, kx), (v, vx)):
            dst[h, 0:EDGE, :] = src[h, pl.ds(low, EDGE), :]
            dst[h, EDGE : EDGE + CHUNK, :] = src[h, 0:CHUNK, :]
            dst[h, EDGE + CHUNK : WIDE, :] = src[h, pl.ds(high, EDGE), :]
        for src, dst in ((q, qx), (ds, dx_)):
            dst[h, 0:EDGE, :] = src[h, pl.ds(low, EDGE), :]
            dst[h, EDGE : 2 * EDGE, :] = src[h, pl.ds(high, EDGE), :]
    low_half, high_half = lax.div(prev, 4), lax.div(nxt, 4)
    low_rows = jnp.where(low_half == 0, stats[place(prev), :, 128:256], stats[place(prev), :, 384:512])
    high_rows = jnp.where(high_half == 0, stats[place(nxt), :, 0:128], stats[place(nxt), :, 256:384])
    low_stats = jnp.transpose(jnp.tile(low_rows, (16, 1)))
    high_stats = jnp.transpose(jnp.tile(high_rows, (16, 1)))
    st[0:EDGE, :] = low_stats[128 - EDGE : 128, :]
    st[EDGE : 2 * EDGE, :] = high_stats[0:EDGE, :]
    def step(dx, carry):
        row = place(dx)
        res = []
        for h in range(OWN_HEADS):
            acc_k, acc_v = carry[2 * h], carry[2 * h + 1]
            for dz in range(2):
                at = pl.multiple_of((dz * 4 + dx) * CHUNK, CHUNK)
                qc = q[h, pl.ds(at, CHUNK), :]
                dc = ds[h, pl.ds(at, CHUNK), :]
                lanes = slice(dz * CHUNK, (dz + 1) * CHUNK)
                log_total = stats[row, h : h + 1, lanes]
                delta = stats[row, h + OWN_HEADS : h + OWN_HEADS + 1, lanes]
                p = jnp.exp2(nt(kx[h], qc) * (SCALE * LOG2E) - log_total * LOG2E)
                acc_v = acc_v + nn(p.astype(BF16), dc)
                dsc = (p * (nt(vx[h], dc) - delta)).astype(BF16)
                acc_k = acc_k + nn(dsc, qc)
            res += [acc_k, acc_v]
        return tuple(res)

    zero = jnp.zeros((WIDE, HEAD_DIM), F32)
    sums = lax.fori_loop(0, 4, step, (zero,) * 6)
    for h in range(OWN_HEADS):
        acc_k, acc_v = sums[2 * h], sums[2 * h + 1]
        p = jnp.exp(nt(qx[h], k[h]) * SCALE - st[:, h : h + 1])
        dsc = (p * (nt(dx_[h], v[h]) - st[:, h + OWN_HEADS : h + OWN_HEADS + 1])).astype(BF16)
        dqx = (nn(dsc, k[h]) * SCALE).astype(BF16)
        cols = slice(h * 128, (h + 1) * 128)
        gs[0:EDGE, cols] = dqx[0:EDGE]
        gs[EDGE : EDGE + CHUNK, cols] = dq[h]
        gs[EDGE + CHUNK : WIDE, cols] = dqx[EDGE : 2 * EDGE]
        gs[:, HALF + h * 128 : HALF + (h + 1) * 128] = (acc_k * SCALE).astype(BF16)
        gs[:, 2 * HALF + h * 128 : 2 * HALF + (h + 1) * 128] = acc_v.astype(BF16)
    mine[...] = gs[pl.ds(pl.multiple_of(core * BLOCK, BLOCK), WINDOW), :]
    give[...] = gs[pl.ds(pl.multiple_of((1 - core) * BLOCK, BLOCK), WINDOW), :]


def conv_body(pos, mine, recv, w_own, w_oth, ext, taps, out, usum, ns, gh, gc):
    _, _, prev_ok, nxt_ok = neighbours(pos, jnp.int32(0), jnp.int32(0))
    first = pos[2] == 0
    low_ok = jnp.where(first, prev_ok, 1.0)
    high_ok = jnp.where(first, 1.0, nxt_ok)
    g = taps[5:6, :]
    for r in range(0, WINDOW, 16):
        ns[r : r + 16, :] = normalize(ext[r : r + 16, :].astype(F32))
    gh[...] = nt(mine[...], w_own[...]) + nt(recv[...], w_oth[...])
    for j in range(0, C, 128):
        tap = [taps[t : t + 1, j : j + 128] for t in range(5)]
        gj = g[:, j : j + 128]
        cols = slice(j, j + 128)

        def grad(r, n):
            near = [ns[r - 2 + t : r - 2 + t + n, cols] for t in range(5)]
            u = tap[0] * (near[0] * gj)
            for t in range(1, 5):
                u = u + tap[t] * (near[t] * gj)
            inner = GELU_ROOT * (u + 0.044715 * u * u * u)
            th = jnp.tanh(inner)
            slope = 0.5 * (1.0 + th) + 0.5 * u * (1.0 - th * th) * GELU_ROOT * (
                1.0 + 3.0 * 0.044715 * u * u
            )
            return near, gh[r : r + n, cols] * slope

        _, edge = grad(8, 8)
        gc[8:16, cols] = edge * low_ok
        _, edge = grad(144, 8)
        gc[144:152, cols] = edge * high_ok
        sums = [jnp.zeros((8, 128), F32) for _ in range(5)]
        for r in range(EDGE, EDGE + BLOCK, 64):
            near, val = grad(r, 64)
            gc[r : r + 64, cols] = val
            for t in range(5):
                sums[t] = sums[t] + jnp.sum((val * near[t]).reshape(8, 8, 128), axis=0)
        side, slot = divmod(j // 128, OWN_HEADS)
        for t in range(5):
            row = t * OWN_HEADS + slot
            usum[side, row : row + 1, :] = jnp.sum(sums[t], axis=0, keepdims=True)
    usum[:, 15:16, :] = jnp.zeros((2, 1, 128), F32)
    tap = [taps[t : t + 1, :] for t in range(5)]
    for r in range(EDGE, EDGE + BLOCK, 16):
        gn = tap[0] * gc[r + 2 : r + 18, :]
        for t in range(1, 5):
            gn = gn + tap[t] * gc[r + 2 - t : r + 18 - t, :]
        x = ext[r : r + 16, :].astype(F32)
        inv = lax.rsqrt(jnp.mean(x * x, axis=-1, keepdims=True) + EPSILON)
        scaled = gn * g
        inner = jnp.mean(scaled * x, axis=-1, keepdims=True)
        res = gh[r : r + 16, :] + inv * scaled - x * (inv * inv * inv * inner)
        out[r - EDGE : r - EDGE + 16, :] = res.astype(BF16)


AXES = ("y", "zm", "zl", "zh", "x", "core")


def swap(a, axis):
    return lax.ppermute(a, axis, [(0, 1), (1, 0)])


def from_x(a, step):
    return lax.ppermute(a, "x", [((i + step) % 4, i) for i in range(4)])


def share(a, axes, size):
    wide = jnp.broadcast_to(a[None], (size,) + a.shape)
    return lax.all_to_all(wide, axes, 0, 0)


def shards(signal, norm_gain, conv_taps, w_query, w_key, w_value, cotangent):
    zh = lax.axis_index("zh")
    xi = lax.axis_index("x")
    core = lax.axis_index("core")
    pos = jnp.stack([zh, xi, core]).astype(jnp.int32)
    first = core == 0
    sig = signal[0]
    cot = cotangent[0]
    gain = norm_gain.reshape(1, C)

    def halves(a):
        low, high = a[:, :HALF], a[:, HALF:]
        return jnp.where(first, low, high), jnp.where(first, high, low)

    keep, give = halves(cot)
    got = swap(give, "core")
    cot_own = jnp.concatenate(
        [jnp.where(first, keep, got), jnp.where(first, got, keep)], axis=1
    )
    sig_z = swap(sig, "zh")
    parts = [halves(w) for w in (w_query, w_key, w_value)]
    w_own = jnp.concatenate([p[0] for p in parts], axis=1)
    w_oth = jnp.concatenate([p[1] for p in parts], axis=1)
    coef = jnp.concatenate([conv_taps, gain, jnp.zeros((2, C), F32)], axis=0)
    cots_near = [from_x(cot_own, d) for d in (1, 2, 3)]
    sig_z, cot_own, w_own, w_oth, coef, cots_near = lax.optimization_barrier(
        (sig_z, cot_own, w_own, w_oth, coef, cots_near)
    )
    cot_z = swap(cot_own, "zh")
    near = share(jnp.concatenate([sig, sig_z], axis=0), "x", 4)
    near, cot_z = lax.optimization_barrier((near, cot_z))
    other = swap(near, "core")
    cots = cots_near + [from_x(cot_z, d) for d in (1, 2, 3)]

    head_shape = jax.ShapeDtypeStruct((OWN_HEADS, BINS, HEAD_DIM), BF16)
    q, k, v, ext = call(
        hidden_body,
        (head_shape, head_shape, head_shape, jax.ShapeDtypeStruct((160, C), BF16)),
        (pos, near, other, w_own, coef),
        HID_SCRATCH,
    )
    part = jax.ShapeDtypeStruct((OWN_HEADS, CHUNK, HEAD_DIM), BF16)
    dq, stats = call(
        forward_body,
        (part, jax.ShapeDtypeStruct((8, 2 * CHUNK), F32)),
        (q, k, v, cot_own, cot_z),
        FWD_SCRATCH,
    )
    stats, cots = lax.optimization_barrier((stats, cots))
    stats_all = share(stats, "x", 4)
    grads = jax.ShapeDtypeStruct((WINDOW, 3 * HALF), BF16)
    mine, give = call(
        backward_body,
        (grads, grads),
        (pos, q, k, v, dq, cot_own, cot_z, *cots, stats_all),
        (
            VM((OWN_HEADS, BINS, HEAD_DIM), BF16),
            VM((WIDE, 3 * HALF), BF16),
            VM((OWN_HEADS, WIDE, HEAD_DIM), BF16),
            VM((OWN_HEADS, WIDE, HEAD_DIM), BF16),
            VM((OWN_HEADS, 2 * EDGE, HEAD_DIM), BF16),
            VM((OWN_HEADS, 2 * EDGE, HEAD_DIM), BF16),
            VM((2 * EDGE, 128), F32),
        ),
    )
    recv = swap(give, "core")
    out, usum = call(
        conv_body,
        (jax.ShapeDtypeStruct((BLOCK, C), BF16), jax.ShapeDtypeStruct((2, 16, 128), F32)),
        (pos, mine, recv, w_own, w_oth, ext, coef),
        (VM((WINDOW, C), F32), VM((WINDOW, C), F32), VM((WINDOW, C), F32)),
    )
    wide = jnp.broadcast_to(usum[None], (16, 2, 16, 128)).reshape(32, 16, 128)
    part = jnp.sum(lax.all_to_all(wide, ("y", "x", "core"), 0, 0), axis=0)
    part = share(part.astype(BF16), ("zm", "zl", "zh"), 16).astype(F32)
    part = jnp.sum(part, axis=0)
    usum = lax.all_gather(part, "core", axis=0)[:, :15].reshape(2, 5, HALF)
    usum = jnp.concatenate([usum[0], usum[1]], axis=1)
    grad_taps = usum * gain
    grad_gain = jnp.sum(usum * conv_taps, axis=0)
    return out[None], grad_taps, grad_gain


def solution(mesh):
    shape = (mesh.devices.size // 128, 2, 4, 2, 4, 2)
    fine = Mesh(mesh.devices.reshape(shape), AXES)
    rows = P(("y", "zm", "zl"), ("zh", "x", "core"), None)
    in_specs = (rows, P(), P(), P(), P(), P(), rows)
    out_specs = (rows, P(), P())
    return jax.shard_map(shards, mesh=fine, in_specs=in_specs, out_specs=out_specs, check_vma=False)
```
